32 devices in a mesh: dp: 2 (over y), row: 4 (over z), col: 4 (over x, core).
Axes of the slice: x: 2, y: 2, z: 4, core: 2. Of those that a mesh axis runs over, the one named last changes fastest.
Arguments:
- block_input: bfloat16 [1024, 1024], P(('dp', 'row'), 'col'), may hold values from -6 to 6
- cotangent: bfloat16 [1024, 1024], P(('dp', 'row'), 'col'), may hold values from -6 to 6
- first_gain: float32 [2, 1024], P(None, 'col'), may hold values from 0.1 to 1.9
- first_shift: float32 [2, 1024], P(None, 'col'), may hold values from -1.75 to 1.75
- joined_weight: bfloat16 [2, 1024, 3072], P(None, 'col', 'row'), may hold values from -0.1875 to 0.1875
- query_bias: float32 [2, 1024], P(None, 'row'), may hold values from -3 to 3
- value_bias: float32 [2, 1024], P(None, 'row'), may hold values from -3 to 3
- output_weight: bfloat16 [2, 1024, 1024], P(None, 'row', 'col'), may hold values from -0.75 to 0.75
- output_bias: float32 [2, 1024], P(None, 'col'), may hold values from -1.75 to 1.75
- second_gain: float32 [2, 1024], P(None, 'col'), may hold values from 0.1 to 1.9
- second_shift: float32 [2, 1024], P(None, 'col'), may hold values from -1.75 to 1.75
- upward_weight: bfloat16 [2, 1024, 4096], P(None, 'col', 'row'), may hold values from -0.1875 to 0.1875
- upward_bias: float32 [2, 4096], P(None, 'row'), may hold values from -3 to 3
- downward_weight: bfloat16 [2, 4096, 1024], P(None, 'row', 'col'), may hold values from -0.09375 to 0.09375
- downward_bias: float32 [2, 1024], P(None, 'col'), may hold values from -1.75 to 1.75
Outputs:
- block_output: bfloat16 [1024, 1024], P(('dp', 'row'), 'col')
- input_gradient: float32 [1024, 1024], P(('dp', 'row'), 'col')
- first_gain_gradient: float32 [2, 1024], P(None, 'col')
- first_shift_gradient: float32 [2, 1024], P(None, 'col')
- joined_weight_gradient: float32 [2, 1024, 3072], P(None, 'col', 'row')
- query_bias_gradient: float32 [2, 1024], P(None, 'row')
- value_bias_gradient: float32 [2, 1024], P(None, 'row')
- output_weight_gradient: float32 [2, 1024, 1024], P(None, 'row', 'col')
- output_bias_gradient: float32 [2, 1024], P(None, 'col')
- second_gain_gradient: float32 [2, 1024], P(None, 'col')
- second_shift_gradient: float32 [2, 1024], P(None, 'col')
- upward_weight_gradient: float32 [2, 1024, 4096], P(None, 'col', 'row')
- upward_bias_gradient: float32 [2, 4096], P(None, 'row')
- downward_weight_gradient: float32 [2, 4096, 1024], P(None, 'row', 'col')
- downward_bias_gradient: float32 [2, 1024], P(None, 'col')
The draws below stay inside these ranges and needn't reach their ends.
All inputs are finite; a program needn't handle non-finite values.
Results may differ from the reference program's by a relative error of at most 0.029.
Values may be sent and summed in bfloat16 or wider, within the bound.
No kernel may reach another device: no remote copies, remote signals or barrier semaphores. Data moves between devices by JAX's collectives and lax.ppermute only.
A program may use at most 64 MiB of HBM per device.

```python
import math
import jax
import jax.numpy as jnp
from jax import lax

D = 1024
H = 16
HD = 64
FF = 4096
SEQ_LEN = 128
LAYERS = 2
TOKENS = 1024


def block_scale(key, shape, shards, low, top_value):
    def one(axis_at, parts):
        steps = jax.random.uniform(jax.random.fold_in(jax.random.fold_in(key, 6), axis_at), (parts,), jnp.float32, low / len(shards), top_value / len(shards))
        return jnp.repeat(jnp.exp(steps), shape[axis_at] // parts).reshape((-1,) + (1,) * (len(shape) - axis_at - 1))

    loudness = one(*shards[0])
    for cut in shards[1:]:
        loudness = loudness * one(*cut)
    return loudness


def bell_draw(stream_key, dims, scale, reach, cuts=(), dtype=jnp.bfloat16):
    values = scale * jax.random.normal(stream_key, dims, jnp.float32)
    if cuts:
        values = values * block_scale(stream_key, dims, cuts, -0.22, 0.18)
    return jnp.clip(values, -reach, reach).astype(dtype)


def setup_inputs(seed: int = 0) -> dict:
    streams_of = jax.random.split(jax.random.key(seed), 16)
    return {
        "block_input": bell_draw(streams_of[0], (TOKENS, D), 1.0, 6.0, ((0, 8), (1, 4))),
        "cotangent": bell_draw(streams_of[1], (TOKENS, D), 1.0, 6.0, ((0, 8), (1, 4))),
        "first_gain": jnp.clip(1.0 + 0.18 * jax.random.normal(streams_of[2], (LAYERS, D), jnp.float32), 0.1, 1.9),
        "first_shift": bell_draw(streams_of[3], (LAYERS, D), 0.3, 1.75, ((1, 4),), jnp.float32),
        "joined_weight": bell_draw(streams_of[4], (LAYERS, D, 3 * D), D ** -0.5, 0.1875, ((1, 4), (2, 4))),
        "query_bias": bell_draw(streams_of[5], (LAYERS, D), 0.5, 3.0, ((1, 4),), jnp.float32),
        "value_bias": bell_draw(streams_of[6], (LAYERS, D), 0.5, 3.0, ((1, 4),), jnp.float32),
        "output_weight": bell_draw(streams_of[7], (LAYERS, D, D), (D // 16) ** -0.5, 0.75, ((1, 4), (2, 4))),
        "output_bias": bell_draw(streams_of[8], (LAYERS, D), 0.3, 1.75, ((1, 4),), jnp.float32),
        "second_gain": jnp.clip(1.0 + 0.18 * jax.random.normal(streams_of[9], (LAYERS, D), jnp.float32), 0.1, 1.9),
        "second_shift": bell_draw(streams_of[10], (LAYERS, D), 0.3, 1.75, ((1, 4),), jnp.float32),
        "upward_weight": bell_draw(streams_of[11], (LAYERS, D, FF), D ** -0.5, 0.1875, ((1, 4), (2, 4))),
        "upward_bias": bell_draw(streams_of[12], (LAYERS, FF), 0.5, 3.0, ((1, 4),), jnp.float32),
        "downward_weight": bell_draw(streams_of[13], (LAYERS, FF, D), FF ** -0.5, 0.09375, ((1, 4), (2, 4))),
        "downward_bias": bell_draw(streams_of[14], (LAYERS, D), 0.3, 1.75, ((1, 4),), jnp.float32),
    }


norm_epsilon = 1e-05
gelu_coef = 0.044715
gelu_scale = math.sqrt(2.0 / math.pi)
masked_score = -1e+30

def round_low(values):
    return lax.optimization_barrier(values.astype(jnp.bfloat16)).astype(jnp.float32)

def gelu_value(values):
    inner = gelu_scale * (values + gelu_coef * values * values * values)
    return 0.5 * values * (1.0 + jnp.tanh(inner))

def gelu_slope(values):
    inner = gelu_scale * (values + gelu_coef * values * values * values)
    tangent = jnp.tanh(inner)
    return 0.5 * (1.0 + tangent) + 0.5 * values * (1.0 - tangent * tangent) * gelu_scale * (1.0 + 3.0 * gelu_coef * values * values)

def layer_norm(resid, gain, shift):
    mean = lax.optimization_barrier(jnp.mean(resid, axis=1))
    spread = lax.optimization_barrier(jnp.mean(resid * resid, axis=1)) - mean * mean
    scale = lax.rsqrt(spread + norm_epsilon)
    normed = (resid - mean[:, None]) * scale[:, None]
    return ((normed * gain + shift).astype(jnp.bfloat16), normed, scale)

def norm_back(grad_out, normed, scale, gain):
    grad_normed = grad_out * gain
    first_mean = lax.optimization_barrier(jnp.mean(grad_normed, axis=1))
    second_mean = lax.optimization_barrier(jnp.mean(grad_normed * normed, axis=1))
    grad_resid = scale[:, None] * (grad_normed - first_mean[:, None] - normed * second_mean[:, None])
    return (grad_resid, lax.optimization_barrier(jnp.sum(grad_out * normed, axis=0)), lax.optimization_barrier(jnp.sum(grad_out, axis=0)))

def head_slopes():
    index = jnp.arange(H).astype(jnp.float32)
    return 2.0 ** (-8.0 * (index + 1.0) / H)

def seq_scores(query, keys, slopes):
    scores = jnp.einsum('qhd,khd->hqk', query.astype(jnp.float32), keys.astype(jnp.float32)) * (1.0 / math.sqrt(HD))
    positions = jnp.arange(query.shape[0])
    offset = (positions[None, :] - positions[:, None]).astype(jnp.float32)
    scores = scores + slopes[:, None, None] * offset[None]
    return jnp.where((offset <= 0.0)[None], scores, masked_score)

def seq_probs(query, keys, slopes):
    scores = seq_scores(query, keys, slopes)
    top = lax.optimization_barrier(jnp.max(scores, axis=2, keepdims=True))
    log_total = top + jnp.log(lax.optimization_barrier(jnp.sum(jnp.exp(scores - top), axis=2, keepdims=True)))
    return jnp.exp(scores - log_total)

def seq_forward(query, keys, values, slopes):
    probs = seq_probs(query, keys, slopes)
    mixed = jnp.einsum('hqk,khd->qhd', round_low(probs), values.astype(jnp.float32))
    return mixed.astype(jnp.bfloat16)

def seq_backward(query, keys, values, mixed, grad_mixed, slopes):
    probs = seq_probs(query, keys, slopes)
    grad_wide = grad_mixed.astype(jnp.float32)
    value_sum = jnp.einsum('hqk,qhd->khd', round_low(probs), grad_wide)
    grad_probs = jnp.einsum('qhd,khd->hqk', grad_wide, values.astype(jnp.float32))
    delta = lax.optimization_barrier(jnp.sum(grad_wide * mixed.astype(jnp.float32), axis=2))
    grad_scores = round_low(probs * (grad_probs - jnp.transpose(delta)[:, :, None]))
    grad_query = jnp.einsum('hqk,khd->qhd', grad_scores, keys.astype(jnp.float32)) * (1.0 / math.sqrt(HD))
    grad_keys = jnp.einsum('hqk,qhd->khd', grad_scores, query.astype(jnp.float32)) * (1.0 / math.sqrt(HD))
    return (grad_query.astype(jnp.bfloat16), grad_keys.astype(jnp.bfloat16), value_sum.astype(jnp.bfloat16))

def reference(block_input, cotangent, first_gain, first_shift, joined_weight, query_bias, value_bias, output_weight, output_bias, second_gain, second_shift, upward_weight, upward_bias, downward_weight, downward_bias):
    slopes = head_slopes()
    total = block_input.shape[0]
    sequences = total // SEQ_LEN

    def split_seq(values):
        return values.reshape(sequences, SEQ_LEN, H, HD)

    def forward_items(items):
        return seq_forward(items[0], items[1], items[2], slopes)

    def backward_items(items):
        return seq_backward(items[0], items[1], items[2], items[3], items[4], slopes)
    resid = block_input.astype(jnp.float32)
    saved = []
    for layer in range(LAYERS):
        first_input, first_normed, first_scale = layer_norm(resid, first_gain[layer], first_shift[layer])
        joined = jnp.dot(first_input, joined_weight[layer], preferred_element_type=jnp.float32).reshape(total, H, 3, HD)
        query = (joined[:, :, 0] + query_bias[layer].reshape(H, HD)).astype(jnp.bfloat16)
        keys = joined[:, :, 1].astype(jnp.bfloat16)
        values = (joined[:, :, 2] + value_bias[layer].reshape(H, HD)).astype(jnp.bfloat16)
        mixed = lax.map(forward_items, (split_seq(query), split_seq(keys), split_seq(values))).reshape(total, D)
        middle = resid + jnp.dot(mixed, output_weight[layer], preferred_element_type=jnp.float32) + output_bias[layer]
        second_input, second_normed, second_scale = layer_norm(middle, second_gain[layer], second_shift[layer])
        pre_act = jnp.dot(second_input, upward_weight[layer], preferred_element_type=jnp.float32) + upward_bias[layer]
        hidden = gelu_value(pre_act).astype(jnp.bfloat16)
        resid = middle + jnp.dot(hidden, downward_weight[layer], preferred_element_type=jnp.float32) + downward_bias[layer]
        saved.append((first_input, first_normed, first_scale, query, keys, values, mixed, second_input, second_normed, second_scale, pre_act, hidden))
    block_output = resid.astype(jnp.bfloat16)
    grad_resid = cotangent.astype(jnp.float32)
    changes = [None] * LAYERS
    for layer in reversed(range(LAYERS)):
        first_input, first_normed, first_scale, query, keys, values, mixed, second_input, second_normed, second_scale, pre_act, hidden = saved[layer]
        grad_low = grad_resid.astype(jnp.bfloat16)
        down_change = jnp.dot(hidden.T, grad_low, preferred_element_type=jnp.float32)
        down_bias_change = lax.optimization_barrier(jnp.sum(grad_resid, axis=0))
        grad_pre = (jnp.dot(grad_low, downward_weight[layer].T, preferred_element_type=jnp.float32) * gelu_slope(pre_act)).astype(jnp.bfloat16)
        up_change = jnp.dot(second_input.T, grad_pre, preferred_element_type=jnp.float32)
        up_bias_change = lax.optimization_barrier(jnp.sum(grad_pre.astype(jnp.float32), axis=0))
        grad_second = jnp.dot(grad_pre, upward_weight[layer].T, preferred_element_type=jnp.float32)
        grad_norm, second_gain_change, second_shift_change = norm_back(grad_second, second_normed, second_scale, second_gain[layer])
        grad_middle = grad_resid + grad_norm
        grad_middle_low = grad_middle.astype(jnp.bfloat16)
        output_change = jnp.dot(mixed.T, grad_middle_low, preferred_element_type=jnp.float32)
        output_bias_change = lax.optimization_barrier(jnp.sum(grad_middle, axis=0))
        grad_mixed = jnp.dot(grad_middle_low, output_weight[layer].T, preferred_element_type=jnp.float32).astype(jnp.bfloat16)
        grad_query, grad_keys, grad_values = lax.map(backward_items, (split_seq(query), split_seq(keys), split_seq(values), split_seq(mixed), split_seq(grad_mixed)))
        grad_joined = jnp.stack([grad_query.reshape(total, H, HD), grad_keys.reshape(total, H, HD), grad_values.reshape(total, H, HD)], axis=2).reshape(total, 3 * D)
        joined_change = jnp.dot(first_input.T, grad_joined, preferred_element_type=jnp.float32)
        per_head = lax.optimization_barrier(jnp.sum(grad_joined.astype(jnp.float32).reshape(total, H, 3, HD), axis=0))
        query_bias_change = per_head[:, 0].reshape(D)
        value_bias_change = per_head[:, 2].reshape(D)
        grad_first = jnp.dot(grad_joined, joined_weight[layer].T, preferred_element_type=jnp.float32)
        grad_norm, first_gain_change, first_shift_change = norm_back(grad_first, first_normed, first_scale, first_gain[layer])
        grad_resid = grad_middle + grad_norm
        changes[layer] = (first_gain_change, first_shift_change, joined_change, query_bias_change, value_bias_change, output_change, output_bias_change, second_gain_change, second_shift_change, up_change, up_bias_change, down_change, down_bias_change)
    stacked = [jnp.stack([changes[layer][slot] for layer in range(LAYERS)], axis=0) for slot in range(13)]
    return (block_output, grad_resid, stacked[0], stacked[1], stacked[2], stacked[3], stacked[4], stacked[5], stacked[6], stacked[7], stacked[8], stacked[9], stacked[10], stacked[11], stacked[12])
```

```python
import math

import jax
import jax.numpy as jnp
from jax import lax
from jax.experimental import pallas as pl
from jax.experimental.pallas import tpu as pltpu
from jax.sharding import PartitionSpec as P


H = 16
HD = 64
LAYERS = 2

VMEM_LIMIT = 16 * 1024 * 1024

norm_epsilon = 1e-05
gelu_coef = 0.044715
gelu_scale = math.sqrt(2.0 / math.pi)
masked_score = -1e30


def int_log2(value):
    return value.bit_length() - 1


def axis_swap(local, axis, step):
    size = lax.axis_size(axis)
    return lax.ppermute(local, axis, [(place, place ^ step) for place in range(size)])


def spread(local, axis):
    size = lax.axis_size(axis)
    return [local] + [axis_swap(local, axis, step) for step in range(1, size)]


def trade(blocks, axis):
    return [blocks[0]] + [axis_swap(blocks[step], axis, step) for step in range(1, len(blocks))]


def relay(sends, axis):
    size = lax.axis_size(axis)
    got = {}
    step = size // 2
    while step:
        arrived = {place ^ step: axis_swap(got[place], axis, step) for place in sorted(got)}
        arrived[step] = axis_swap(sends[step], axis, step)
        got.update(arrived)
        step //= 2
    return [got[place] for place in range(1, size)]


def sends_of(size):
    steps = []
    step = 1
    while step < size:
        steps.append(step)
        step *= 2
    return steps


def relay_all(local, axis):
    return [local] + relay({step: local for step in sends_of(lax.axis_size(axis))}, axis)


def high_bit(place):
    return 1 << int_log2(place)


def tree_sum(parts):
    parts = list(parts)
    while len(parts) > 1:
        parts = [parts[at] + parts[at + 1] for at in range(0, len(parts), 2)]
    return parts[0]


def dot(left, right):
    return lax.dot_general(left, right, (((1,), (0,)), ((), ())), preferred_element_type=jnp.float32)


def dot_right(left, right):
    return lax.dot_general(left, right, (((1,), (1,)), ((), ())), preferred_element_type=jnp.float32)


def dot_left(left, right):
    return lax.dot_general(left, right, (((0,), (0,)), ((), ())), preferred_element_type=jnp.float32)


def low(values):
    return values.astype(jnp.bfloat16)


def wide(values):
    return values.astype(jnp.float32)


def shaped(shape, dtype):
    return jax.ShapeDtypeStruct(shape, dtype)


BF = jnp.bfloat16
F32 = jnp.float32


SMEM = pl.BlockSpec(memory_space=pltpu.SMEM)
VMEM = pl.BlockSpec(memory_space=pltpu.VMEM)
ANY = pl.BlockSpec(memory_space=pl.ANY)


def run(kernel, scalars, arrays, outs, scratch=()):
    return pl.pallas_call(
        kernel,
        in_specs=[SMEM] * len(scalars) + [VMEM] * len(arrays),
        out_specs=[VMEM] * len(outs),
        out_shape=outs,
        scratch_shapes=list(scratch),
        compiler_params=pltpu.CompilerParams(vmem_limit_bytes=VMEM_LIMIT),
    )(*scalars, *arrays)


def vector_row(vecs, at):
    return jnp.concatenate([vec[at : at + 1, :] for vec in vecs], axis=1)


def norm_into(resid, gain, shift, input_ref, normed_ref, scale_ref):
    mean = jnp.mean(resid, axis=1, keepdims=True)
    spread_out = jnp.mean(resid * resid, axis=1, keepdims=True) - mean * mean
    scale = lax.rsqrt(spread_out + norm_epsilon)
    normed = (resid - mean) * scale
    normed_ref[...] = normed
    scale_ref[...] = jnp.broadcast_to(scale, scale_ref.shape)
    input_ref[...] = low(normed * gain + shift)


def start_blocks(block_input, cotangent, vectors, size):
    rows = block_input.shape[0] // size
    width = block_input.shape[1]

    def kernel(input_ref, cotangent_ref, *refs):
        vector_refs = refs[: len(vectors)]
        outs = refs[len(vectors) :]
        for step in range(size):
            outs[step][:, :width] = input_ref[step * rows : (step + 1) * rows, :]
            outs[step][:, width:] = cotangent_ref[step * rows : (step + 1) * rows, :]
        for at, ref in enumerate(vector_refs):
            outs[size][LAYERS * at : LAYERS * (at + 1), :] = ref[...]

    outs = run(
        kernel,
        [],
        [block_input, cotangent, *vectors],
        [shaped((rows, 2 * width), BF)] * size + [shaped((LAYERS * len(vectors), width), F32)],
    )
    return outs[:size], outs[size]


def turn_blocks(blocks, place):
    size = len(blocks)

    def kernel(place_ref, *refs):
        block_refs, out_refs, turn = refs[:size], refs[size : 2 * size], refs[2 * size]
        for at in range(size):
            turn[at] = block_refs[at][...]
        for at in range(size):
            out_refs[at][...] = turn[at ^ place_ref[0] ^ place_ref[1]]

    shape, dtype = blocks[0].shape, blocks[0].dtype
    return run(
        kernel,
        [place],
        list(blocks),
        [shaped(shape, dtype)] * size,
        [pltpu.VMEM((size,) + shape, dtype)],
    )


def pack_weights(joined, output, upward, downward, layer, first):
    width = joined.shape[1]
    pieces = []
    if first:
        pieces.append((0, (layer, slice(None)), joined.shape[2]))
        pieces.append((1, (layer, slice(None)), output.shape[2]))
        arrays = [joined, output]
    else:
        pieces.append((0, (layer, slice(None)), upward.shape[2]))
        for at in range(downward.shape[1] // width):
            pieces.append((1, (layer, slice(at * width, (at + 1) * width)), downward.shape[2]))
        arrays = [upward, downward]
    total = sum(piece[2] for piece in pieces)

    def kernel(one_ref, two_ref, out_ref, sems):
        copies = []
        at = 0
        for slot, (which, index, columns) in enumerate(pieces):
            ref = (one_ref, two_ref)[which]
            copies.append(
                pltpu.make_async_copy(
                    ref.at[index], out_ref.at[:, at : at + columns], sems.at[slot]
                )
            )
            at += columns
        for copy in copies:
            copy.start()
        for copy in copies:
            copy.wait()

    return pl.pallas_call(
        kernel,
        name="pack_weights",
        in_specs=[ANY] * 2,
        out_specs=ANY,
        out_shape=shaped((width, total), BF),
        scratch_shapes=[pltpu.SemaphoreType.DMA((len(pieces),))],
        compiler_params=pltpu.CompilerParams(vmem_limit_bytes=VMEM_LIMIT),
    )(*arrays)


def first_norm(got, vecs):
    size = len(got)
    rows, width = got[0].shape[0], got[0].shape[1] // 2

    def kernel(*refs):
        got_refs = refs[:size]
        vec_refs = refs[size : size + len(vecs)]
        resid_ref, cotangent_ref, input_ref, normed_ref, scale_ref = refs[size + len(vecs) :]
        whole = [ref[...] for ref in got_refs]
        resid = jnp.concatenate([wide(part[:, :width]) for part in whole], axis=1)
        cotangent_ref[...] = jnp.concatenate([part[:, width:] for part in whole], axis=1)
        resid_ref[...] = resid
        norm_into(
            resid,
            vector_row(vec_refs, GAIN_ONE * LAYERS),
            vector_row(vec_refs, SHIFT_ONE * LAYERS),
            input_ref,
            normed_ref,
            scale_ref,
        )

    full = size * width
    return run(
        kernel,
        [],
        [*got, *vecs],
        [
            shaped((rows, full), F32),
            shaped((rows, full), BF),
            shaped((rows, full), BF),
            shaped((rows, full), F32),
            shaped((rows, 128), F32),
        ],
    )


def next_norm(resid, parts, vecs, layer, bias_at, gain_at, shift_at):
    count = len(parts)
    next_layer = layer + 1 if gain_at == GAIN_ONE else layer

    def kernel(resid_ref, *refs):
        part_refs = refs[:count]
        vec_refs = refs[count : count + len(vecs)]
        out_ref, input_ref, normed_ref, scale_ref = refs[count + len(vecs) :]
        total = tree_sum([wide(ref[...]) for ref in part_refs])
        resid = resid_ref[...] + total + vector_row(vec_refs, bias_at * LAYERS + layer)
        out_ref[...] = resid
        norm_into(
            resid,
            vector_row(vec_refs, gain_at * LAYERS + next_layer),
            vector_row(vec_refs, shift_at * LAYERS + next_layer),
            input_ref,
            normed_ref,
            scale_ref,
        )

    rows, full = resid.shape
    return run(
        kernel,
        [],
        [resid, *parts, *vecs],
        [
            shaped((rows, full), F32),
            shaped((rows, full), BF),
            shaped((rows, full), F32),
            shaped((rows, 128), F32),
        ],
    )


def cut_rows(value, refs):
    rows = refs[0].shape[0]
    for at, ref in enumerate(refs):
        ref[...] = value[at * rows : (at + 1) * rows]


def cut_columns(value, refs):
    width = refs[0].shape[1]
    for at, ref in enumerate(refs):
        ref[...] = value[:, at * width : (at + 1) * width]


def gathered(refs):
    return jnp.concatenate([ref[...] for ref in refs], axis=0)


def attention_forward(blocks, packs, query_bias, value_bias, slopes, place, layer):
    size, cols = len(blocks), len(packs)
    rows, full = blocks[0].shape
    length = size * rows
    width = full // cols
    across = query_bias.shape[1]
    heads = across // HD
    shift = int_log2(rows)

    def kernel(place_ref, slopes_ref, *refs):
        block_refs = refs[:size]
        pack_refs = refs[size : size + cols]
        query_bias_ref, value_bias_ref = refs[size + cols : size + cols + 2]
        all_ref, qkv_ref, probs_ref, mixed_ref = refs[size + cols + 2 : size + cols + 6]
        part_refs = refs[size + cols + 6 :]
        full_first = gathered(block_refs)
        all_ref[...] = full_first
        joined = tree_sum(
            [
                dot(full_first[:, at * width : (at + 1) * width], pack_refs[at][:, : 3 * across])
                for at in range(cols)
            ]
        )
        turn = place_ref[0] ^ place_ref[1]

        def where_is(axis):
            index = lax.broadcasted_iota(jnp.int32, (length, length), axis)
            return ((lax.shift_right_logical(index, shift) ^ turn) << shift) + (index & (rows - 1))

        offset = wide(where_is(1) - where_is(0))
        allowed = offset <= 0.0
        for head in range(heads):
            at = head * 3 * HD
            here = slice(head * HD, (head + 1) * HD)
            query = low(joined[:, at : at + HD] + query_bias_ref[layer : layer + 1, here])
            keys = low(joined[:, at + HD : at + 2 * HD])
            values = low(
                joined[:, at + 2 * HD : at + 3 * HD] + value_bias_ref[layer : layer + 1, here]
            )
            qkv_ref[:, at : at + HD] = query
            qkv_ref[:, at + HD : at + 2 * HD] = keys
            qkv_ref[:, at + 2 * HD : at + 3 * HD] = values
            scores = dot_right(query, keys) * (1.0 / math.sqrt(HD)) + slopes_ref[head] * offset
            scores = jnp.where(allowed, scores, masked_score)
            top = jnp.max(scores, axis=1, keepdims=True)
            log_total = top + jnp.log(jnp.sum(jnp.exp(scores - top), axis=1, keepdims=True))
            probs = jnp.exp(scores - log_total)
            probs_ref[head] = probs
            mixed_ref[:, here] = low(dot(low(probs), values))
        mixed = mixed_ref[...]
        partial = jnp.concatenate(
            [low(dot(mixed, pack_ref[:, 3 * across : 3 * across + width])) for pack_ref in pack_refs],
            axis=1,
        )
        cut_rows(partial, part_refs)

    outs = run(
        kernel,
        [place, slopes],
        [*blocks, *packs, query_bias, value_bias],
        [
            shaped((length, full), BF),
            shaped((length, 3 * across), BF),
            shaped((heads, length, length), F32),
            shaped((length, across), BF),
        ]
        + [shaped((rows, full), BF)] * size,
    )
    return outs[:4], outs[4:]


def bundle_into(refs, steps, shared, addressed, width):
    for at, ref in enumerate(refs):
        first = steps[at - 1] if at else 0
        count = first if at else 1
        column = 0
        for value in shared:
            ref[:, column : column + value.shape[1]] = value
            column += value.shape[1]
        for place in range(first, first + count):
            for value in addressed:
                ref[:, column : column + width] = value[:, place * width : (place + 1) * width]
                column += width


def bundle_shapes(length, steps, shared, addressed, width):
    counts = [1] + list(steps)
    return [shaped((length, shared + count * addressed * width), BF) for count in counts]


def feed_forward(blocks, packs, upward_bias, first_all, mixed, layer):
    size, cols = len(blocks), len(packs)
    rows, full = blocks[0].shape
    length = size * rows
    width = full // cols
    units = upward_bias.shape[1]
    across = mixed.shape[1]
    steps = sends_of(cols)

    def kernel(*refs):
        block_refs = refs[:size]
        pack_refs = refs[size : size + cols]
        bias_ref, first_ref, mixed_ref, slope_ref = refs[size + cols : size + cols + 4]
        part_refs = refs[size + cols + 4 : 2 * size + cols + 4]
        send_refs = refs[2 * size + cols + 4 :]
        full_second = gathered(block_refs)
        pre_act = tree_sum(
            [
                dot(full_second[:, at * width : (at + 1) * width], pack_refs[at][:, :units])
                for at in range(cols)
            ]
        )
        pre_act = pre_act + bias_ref[layer : layer + 1, :]
        inner = gelu_scale * (pre_act + gelu_coef * pre_act * pre_act * pre_act)
        tangent = jnp.tanh(inner)
        hidden = low(0.5 * pre_act * (1.0 + tangent))
        slope_ref[...] = 0.5 * (1.0 + tangent) + 0.5 * pre_act * (
            1.0 - tangent * tangent
        ) * gelu_scale * (1.0 + 3.0 * gelu_coef * pre_act * pre_act)
        partial = jnp.concatenate(
            [
                low(
                    tree_sum(
                        [
                            dot(
                                hidden[:, at : at + width],
                                pack_ref[:, units + at : units + at + width],
                            )
                            for at in range(0, units, width)
                        ]
                    )
                )
                for pack_ref in pack_refs
            ],
            axis=1,
        )
        cut_rows(partial, part_refs)
        bundle_into(
            send_refs, steps, [mixed_ref[...], hidden], [first_ref[...], full_second], width
        )

    outs = run(
        kernel,
        [],
        [*blocks, *packs, upward_bias, first_all, mixed],
        [shaped((length, units), F32)]
        + [shaped((rows, full), BF)] * size
        + bundle_shapes(length, steps, across + units, 2, width),
    )
    return outs[0], outs[1 : 1 + size], outs[1 + size :]


def feed_backward(blocks, packs, slope):
    size, cols = len(blocks), len(packs)
    rows, full = blocks[0].shape
    length = size * rows
    width = full // cols
    units = slope.shape[1]
    steps = sends_of(cols)

    def kernel(*refs):
        block_refs = refs[:size]
        pack_refs = refs[size : size + cols]
        slope_ref = refs[size + cols]
        part_refs = refs[size + cols + 1 : 2 * size + cols + 1]
        send_refs = refs[2 * size + cols + 1 :]
        full_grad = gathered(block_refs)
        grad_hidden = jnp.concatenate(
            [
                tree_sum(
                    [
                        dot_right(
                            full_grad[:, place * width : (place + 1) * width],
                            pack_refs[place][:, units + at : units + at + width],
                        )
                        for place in range(cols)
                    ]
                )
                for at in range(0, units, width)
            ],
            axis=1,
        )
        grad_pre = low(grad_hidden * slope_ref[...])
        partial = jnp.concatenate(
            [low(dot_right(grad_pre, pack_ref[:, :units])) for pack_ref in pack_refs], axis=1
        )
        cut_rows(partial, part_refs)
        bundle_into(send_refs, steps, [grad_pre], [full_grad], width)

    outs = run(
        kernel,
        [],
        [*blocks, *packs, slope],
        [shaped((rows, full), BF)] * size + bundle_shapes(length, steps, units, 1, width),
    )
    return outs[:size], outs[size:]


def norm_backward(grad_resid, parts, normed, scale, vecs, layer, gain_at, extra):
    count = len(parts)
    rows, full = grad_resid.shape

    def kernel(grad_ref, normed_ref, scale_ref, *refs):
        part_refs = refs[:count]
        vec_refs = refs[count : count + len(vecs)]
        out_ref, low_ref, sums_ref = refs[count + len(vecs) :]
        grad_in = wide(grad_ref[...])
        grad_out = tree_sum([wide(ref[...]) for ref in part_refs])
        normed = normed_ref[...]
        grad_normed = grad_out * vector_row(vec_refs, gain_at * LAYERS + layer)
        first = jnp.mean(grad_normed, axis=1, keepdims=True)
        second = jnp.mean(grad_normed * normed, axis=1, keepdims=True)
        total = grad_in + scale_ref[:, :1] * (grad_normed - first - normed * second)
        out_ref[...] = total
        low_ref[...] = low(total)
        sums_ref[0:1, :] = jnp.sum(grad_out * normed, axis=0, keepdims=True)
        sums_ref[1:2, :] = jnp.sum(grad_out, axis=0, keepdims=True)
        if extra:
            sums_ref[2:3, :] = jnp.sum(total, axis=0, keepdims=True)
            sums_ref[3:4, :] = jnp.sum(grad_in, axis=0, keepdims=True)

    return run(
        kernel,
        [],
        [grad_resid, normed, scale, *parts, *vecs],
        [
            shaped((rows, full), F32),
            shaped((rows, full), BF),
            shaped((4 if extra else 2, full), F32),
        ],
    )


def attention_backward(blocks, packs, qkv, probs, mixed):
    size, cols = len(blocks), len(packs)
    rows, full = blocks[0].shape
    length = size * rows
    width = full // cols
    across = mixed.shape[1]
    heads = across // HD
    steps = sends_of(cols)
    factor = 1.0 / math.sqrt(HD)

    def kernel(*refs):
        block_refs = refs[:size]
        pack_refs = refs[size : size + cols]
        qkv_ref, probs_ref, mixed_ref = refs[size + cols : size + cols + 3]
        part_refs = refs[size + cols + 3 : 2 * size + cols + 3]
        send_refs = refs[2 * size + cols + 3 :]
        joined_ref = send_refs[0]
        full_middle = gathered(block_refs)
        grad_mixed = low(
            tree_sum(
                [
                    dot_right(
                        full_middle[:, at * width : (at + 1) * width],
                        pack_refs[at][:, 3 * across : 3 * across + width],
                    )
                    for at in range(cols)
                ]
            )
        )
        for head in range(heads):
            at = head * 3 * HD
            here = slice(head * HD, (head + 1) * HD)
            query = qkv_ref[:, at : at + HD]
            keys = qkv_ref[:, at + HD : at + 2 * HD]
            values = qkv_ref[:, at + 2 * HD : at + 3 * HD]
            grad_here = grad_mixed[:, here]
            probs = probs_ref[head]
            value_sum = dot_left(low(probs), grad_here)
            grad_probs = dot_right(grad_here, values)
            delta = jnp.sum(wide(grad_here) * wide(mixed_ref[:, here]), axis=1, keepdims=True)
            grad_scores = low(probs * (grad_probs - delta))
            joined_ref[:, at : at + HD] = low(dot(grad_scores, keys) * factor)
            joined_ref[:, at + HD : at + 2 * HD] = low(dot_left(grad_scores, query) * factor)
            joined_ref[:, at + 2 * HD : at + 3 * HD] = low(value_sum)
        grad_joined = joined_ref[:, : 3 * across]
        partial = jnp.concatenate(
            [low(dot_right(grad_joined, pack_ref[:, : 3 * across])) for pack_ref in pack_refs],
            axis=1,
        )
        cut_rows(partial, part_refs)
        bundle_into(send_refs, steps, [grad_joined], [full_middle], width)

    outs = run(
        kernel,
        [],
        [*blocks, *packs, qkv, probs, mixed],
        [shaped((rows, full), BF)] * size + bundle_shapes(length, steps, 3 * across, 1, width),
    )
    return outs[:size], outs[size:]


def columns_of(place, slot, shared, addressed, width):
    index = place - high_bit(place) if place else 0
    start = shared + (index * addressed + slot) * width
    return slice(start, start + width)


def feed_changes(ahead, behind, across, units, width):
    cols = len(ahead)
    shared = across + units

    def kernel(*refs):
        ahead_refs = refs[:cols]
        behind_refs = refs[cols : 2 * cols]
        out_ref, sum_ref = refs[2 * cols :]

        def rows_of(some, pick):
            return jnp.concatenate([ref[:, pick(at)] for at, ref in enumerate(some)], axis=0)

        grad_all = rows_of(behind_refs, lambda at: columns_of(at, 0, units, 1, width))
        pre_all = rows_of(behind_refs, lambda at: slice(0, units))
        second_all = rows_of(ahead_refs, lambda at: columns_of(at, 1, shared, 2, width))
        out_ref[:, :units] = low(dot_left(second_all, pre_all))
        for at in range(0, units, width):
            hidden_all = rows_of(ahead_refs, lambda _: slice(across + at, across + at + width))
            out_ref[:, units + at : units + at + width] = low(dot_left(hidden_all, grad_all))
        sum_ref[...] = jnp.sum(wide(pre_all), axis=0, keepdims=True)

    return run(
        kernel, [], [*ahead, *behind], [shaped((width, 2 * units), BF), shaped((1, units), F32)]
    )


def attention_changes(ahead, behind, across, units, width):
    cols = len(ahead)
    shared = across + units

    def kernel(*refs):
        ahead_refs = refs[:cols]
        behind_refs = refs[cols : 2 * cols]
        out_ref, sum_ref = refs[2 * cols :]

        def rows_of(some, pick):
            return jnp.concatenate([ref[:, pick(at)] for at, ref in enumerate(some)], axis=0)

        first_all = rows_of(ahead_refs, lambda at: columns_of(at, 0, shared, 2, width))
        joined_all = rows_of(behind_refs, lambda at: slice(0, 3 * across))
        middle_all = rows_of(behind_refs, lambda at: columns_of(at, 0, 3 * across, 1, width))
        mixed_all = rows_of(ahead_refs, lambda at: slice(0, across))
        out_ref[:, : 3 * across] = low(dot_left(first_all, joined_all))
        out_ref[:, 3 * across :] = low(dot_left(mixed_all, middle_all))
        sum_ref[...] = jnp.sum(wide(joined_all), axis=0, keepdims=True)

    return run(
        kernel,
        [],
        [*ahead, *behind],
        [shaped((width, 3 * across + width), BF), shaped((1, 3 * across), F32)],
    )


def finish(own, other, layer, cuts, shapes, kept):
    def kernel(own_ref, other_ref, *refs):
        out_refs = refs[len(kept or ()) :]
        for out_ref, pieces in zip(out_refs, cuts):
            row = 0
            for start, stop in pieces:
                out_ref[0, row : row + own_ref.shape[0], :] = wide(own_ref[:, start:stop]) + wide(
                    other_ref[:, start:stop]
                )
                row += own_ref.shape[0]

    def whole(array):
        return pl.BlockSpec(array.shape, lambda at: (0, 0))

    return pl.pallas_call(
        kernel,
        name="finish",
        grid=(1,),
        in_specs=[whole(own), whole(other)] + [ANY] * len(kept or ()),
        out_specs=[pl.BlockSpec((1,) + shape[1:], lambda at: (layer, 0, 0)) for shape in shapes],
        out_shape=[shaped(shape, F32) for shape in shapes],
        input_output_aliases={2 + at: at for at in range(len(kept or ()))},
        compiler_params=pltpu.CompilerParams(vmem_limit_bytes=VMEM_LIMIT),
    )(own, other, *(kept or ()))


def end_blocks(values, size):
    rows, full = values.shape
    width = full // size

    def kernel(value_ref, *out_refs):
        for at in range(size):
            out_refs[at][...] = value_ref[:, at * width : (at + 1) * width]

    return run(kernel, [], [values], [shaped((rows, width), values.dtype)] * size)


def end_place(got):
    size = len(got)
    rows, width = got[0].shape

    def kernel(*refs):
        cut = refs[size]
        for at in range(size):
            cut[at * rows : (at + 1) * rows, :] = refs[at][...]

    return run(kernel, [], list(got), [shaped((rows * size, width), got[0].dtype)])[0]


def turn_in(blocks, place):
    got = turn_blocks(trade(blocks, "row"), place)
    return trade(got, "col")


def turn_out(blocks, place):
    got = turn_blocks(trade(blocks, "col"), place)
    return end_place(trade(got, "row"))


def width_total(vectors):
    size = lax.axis_size("col")
    share = vectors.shape[1] // size
    step = size // 2
    while step:
        mine, theirs = vectors[:, : step * share], vectors[:, step * share :]
        vectors = mine + axis_swap(theirs, "col", step)
        step //= 2
    return over_dp(tree_sum(spread(vectors, "row")))


def over_dp(total):
    step = lax.axis_size("dp") // 2
    while step:
        total = total + axis_swap(total, "dp", step)
        step //= 2
    return total


def last_resid(resid, parts, vecs, layer):
    count = len(parts)

    def kernel(resid_ref, *refs):
        part_refs = refs[:count]
        vec_refs = refs[count : count + len(vecs)]
        total = tree_sum([wide(ref[...]) for ref in part_refs])
        bias = vector_row(vec_refs, BIAS_DOWN * LAYERS + layer)
        cut_columns(low(resid_ref[...] + total + bias), refs[count + len(vecs) :])

    rows, full = resid.shape
    width = full // len(vecs)
    return run(kernel, [], [resid, *parts, *vecs], [shaped((rows, width), BF)] * len(vecs))


GAIN_ONE, SHIFT_ONE, BIAS_OUT, GAIN_TWO, SHIFT_TWO, BIAS_DOWN = range(6)


def shards(
    block_input,
    cotangent,
    first_gain,
    first_shift,
    joined_weight,
    query_bias,
    value_bias,
    output_weight,
    output_bias,
    second_gain,
    second_shift,
    upward_weight,
    upward_bias,
    downward_weight,
    downward_bias,
):
    row = lax.axis_index("row")
    col = lax.axis_index("col")
    place = jnp.stack([row, col]).astype(jnp.int32)
    across = query_bias.shape[1]
    heads_here = across // HD
    units = upward_bias.shape[1]
    width = block_input.shape[1]
    size = lax.axis_size("row")
    steps = sends_of(lax.axis_size("col"))
    head_index = (row * heads_here).astype(jnp.float32) + jnp.arange(heads_here).astype(jnp.float32)
    slopes = 2.0 ** (-8.0 * (head_index + 1.0) / H)

    blocks, vectors = start_blocks(
        block_input,
        cotangent,
        [first_gain, first_shift, output_bias, second_gain, second_shift, downward_bias],
        size,
    )
    got = turn_in(blocks, place)
    vecs = relay_all(vectors, "col")
    weights = []
    for layer in range(LAYERS):
        weights.append([])
        for first in (True, False):
            pack = pack_weights(
                joined_weight, output_weight, upward_weight, downward_weight, layer, first
            )
            weights[layer].append(relay_all(pack, "col"))
    resid, grad_resid, norm_input, normed, scale = first_norm(got, vecs)
    saved = []
    for layer in range(LAYERS):
        attention_packs, feed_packs = weights[layer]
        first_kept = (normed, scale)
        (first_all, qkv, probs, mixed), parts = attention_forward(
            spread(norm_input, "row"), attention_packs, query_bias, value_bias, slopes, place, layer
        )
        middle, norm_input, normed, scale = next_norm(
            resid, trade(parts, "row"), vecs, layer, BIAS_OUT, GAIN_TWO, SHIFT_TWO
        )
        slope, parts, sends = feed_forward(
            spread(norm_input, "row"), feed_packs, upward_bias, first_all, mixed, layer
        )
        ahead = [sends[0]] + relay(dict(zip(steps, sends[1:])), "col")
        saved.append((first_kept, (normed, scale), qkv, probs, mixed, slope, ahead))
        parts = trade(parts, "row")
        if layer + 1 < LAYERS:
            resid, norm_input, normed, scale = next_norm(
                middle, parts, vecs, layer, BIAS_DOWN, GAIN_ONE, SHIFT_ONE
            )
        else:
            block_output = turn_out(last_resid(middle, parts, vecs, layer), place)

    grad_low = grad_resid
    sums = [None] * LAYERS
    lines = [None] * LAYERS
    feed_outs = attention_outs = None
    for layer in reversed(range(LAYERS)):
        attention_packs, feed_packs = weights[layer]
        first_kept, second_kept, qkv, probs, mixed, slope, ahead = saved[layer]
        parts, sends = feed_backward(spread(grad_low, "row"), feed_packs, slope)
        feed_behind = [sends[0]] + relay(dict(zip(steps, sends[1:])), "col")
        grad_middle, middle_low, second_sums = norm_backward(
            grad_resid, trade(parts, "row"), *second_kept, vecs, layer, GAIN_TWO, True
        )
        parts, sends = attention_backward(
            spread(middle_low, "row"), attention_packs, qkv, probs, mixed
        )
        attention_behind = [sends[0]] + relay(dict(zip(steps, sends[1:])), "col")
        grad_resid, grad_low, first_sums = norm_backward(
            grad_middle, trade(parts, "row"), *first_kept, vecs, layer, GAIN_ONE, False
        )
        change, pre_sum = feed_changes(ahead, feed_behind, across, units, width)
        feed_outs = finish(
            change,
            axis_swap(change, "dp", 1),
            layer,
            [[(0, units)], [(at, at + width) for at in range(units, 2 * units, width)]],
            [upward_weight.shape, downward_weight.shape],
            feed_outs,
        )
        change, joined_sum = attention_changes(ahead, attention_behind, across, units, width)
        attention_outs = finish(
            change,
            axis_swap(change, "dp", 1),
            layer,
            [[(0, 3 * across)], [(3 * across, 3 * across + width)]],
            [joined_weight.shape, output_weight.shape],
            attention_outs,
        )
        sums[layer] = (first_sums, second_sums)
        lines[layer] = (pre_sum, joined_sum)
    input_gradient = turn_out(end_blocks(grad_resid, size), place)
    vector_sums = width_total(
        jnp.concatenate([part for pair in sums for part in pair], axis=0)
    ).reshape(LAYERS, 6, width)
    line = over_dp(jnp.concatenate([part for pair in lines for part in pair], axis=1))
    line = line.reshape(LAYERS, units + 3 * across)
    per_head = line[:, units:].reshape(LAYERS, heads_here, 3, HD)
    return (
        block_output,
        input_gradient,
        vector_sums[:, 0],
        vector_sums[:, 1],
        attention_outs[0],
        per_head[:, :, 0].reshape(LAYERS, across),
        per_head[:, :, 2].reshape(LAYERS, across),
        attention_outs[1],
        vector_sums[:, 4],
        vector_sums[:, 2],
        vector_sums[:, 3],
        feed_outs[0],
        line[:, :units],
        feed_outs[1],
        vector_sums[:, 5],
    )


def solution(mesh):
    return jax.shard_map(
        shards,
        mesh=mesh,
        in_specs=(
            P(("dp", "row"), "col"),
            P(("dp", "row"), "col"),
            P(None, "col"),
            P(None, "col"),
            P(None, "col", "row"),
            P(None, "row"),
            P(None, "row"),
            P(None, "row", "col"),
            P(None, "col"),
            P(None, "col"),
            P(None, "col"),
            P(None, "col", "row"),
            P(None, "row"),
            P(None, "row", "col"),
            P(None, "col"),
        ),
        out_specs=(
            P(("dp", "row"), "col"),
            P(("dp", "row"), "col"),
            P(None, "col"),
            P(None, "col"),
            P(None, "col", "row"),
            P(None, "row"),
            P(None, "row"),
            P(None, "row", "col"),
            P(None, "col"),
            P(None, "col"),
            P(None, "col"),
            P(None, "col", "row"),
            P(None, "row"),
            P(None, "row", "col"),
            P(None, "col"),
        ),
        check_vma=False,
    )
```

```python
import math

import jax
import jax.numpy as jnp
from jax import lax
from jax.experimental import pallas as pl
from jax.experimental.pallas import tpu as pltpu
from jax.sharding import PartitionSpec as P


H = 16
HD = 64
LAYERS = 2

VMEM_LIMIT = 16 * 1024 * 1024
DP, ROW, COL = "dp", "row", "col"
GAIN_ONE, SHIFT_ONE, BIAS_OUT, GAIN_TWO, SHIFT_TWO, BIAS_DOWN = range(6)

norm_epsilon = 1e-05
gelu_coef = 0.044715
gelu_scale = math.sqrt(2.0 / math.pi)
masked_score = -1e30


def int_log2(value):
    return value.bit_length() - 1


def axis_swap(local, axis, step):
    size = lax.axis_size(axis)
    return lax.ppermute(local, axis, [(place, place ^ step) for place in range(size)])


def spread(local, axis):
    size = lax.axis_size(axis)
    return [local] + [axis_swap(local, axis, step) for step in range(1, size)]


def trade(blocks, axis):
    return [blocks[0]] + [axis_swap(blocks[step], axis, step) for step in range(1, len(blocks))]


def relay(sends, axis):
    size = lax.axis_size(axis)
    got = {}
    step = size // 2
    while step:
        arrived = {place ^ step: axis_swap(got[place], axis, step) for place in sorted(got)}
        arrived[step] = axis_swap(sends[step], axis, step)
        got.update(arrived)
        step //= 2
    return [got[place] for place in range(1, size)]


def sends_of(size):
    steps = []
    step = 1
    while step < size:
        steps.append(step)
        step *= 2
    return steps


def relay_all(local, axis):
    return [local] + relay({step: local for step in sends_of(lax.axis_size(axis))}, axis)


def high_bit(place):
    return 1 << int_log2(place)


def tree_sum(parts):
    parts = list(parts)
    while len(parts) > 1:
        parts = [parts[at] + parts[at + 1] for at in range(0, len(parts), 2)]
    return parts[0]


def dot(left, right):
    return lax.dot_general(left, right, (((1,), (0,)), ((), ())), preferred_element_type=jnp.float32)


def dot_right(left, right):
    return lax.dot_general(left, right, (((1,), (1,)), ((), ())), preferred_element_type=jnp.float32)


def dot_left(left, right):
    return lax.dot_general(left, right, (((0,), (0,)), ((), ())), preferred_element_type=jnp.float32)


def low(values):
    return values.astype(jnp.bfloat16)


def wide(values):
    return values.astype(jnp.float32)


def shaped(shape, dtype):
    return jax.ShapeDtypeStruct(shape, dtype)


BF = jnp.bfloat16
F32 = jnp.float32


VMEM = pl.BlockSpec(memory_space=pltpu.VMEM)
ANY = pl.BlockSpec(memory_space=pl.ANY)
HBM = pl.BlockSpec(memory_space=pltpu.HBM)


def run(kernel, arrays, outs, scratch=(), spec=None):
    return pl.pallas_call(
        kernel,
        in_specs=[spec or VMEM] * len(arrays),
        out_specs=[VMEM] * len(outs),
        out_shape=outs,
        scratch_shapes=list(scratch),
        compiler_params=pltpu.CompilerParams(vmem_limit_bytes=VMEM_LIMIT),
    )(*arrays)


def vector_row(vecs, at):
    return jnp.concatenate([vec[at : at + 1, :] for vec in vecs], axis=1)


def norm_into(resid, gain, shift, input_ref, stats_ref):
    mean = jnp.mean(resid, axis=1, keepdims=True)
    spread_out = jnp.mean(resid * resid, axis=1, keepdims=True) - mean * mean
    scale = lax.rsqrt(spread_out + norm_epsilon)
    half = stats_ref.shape[1] // 2
    stats_ref[:, :half] = jnp.broadcast_to(mean, (resid.shape[0], half))
    stats_ref[:, half:] = jnp.broadcast_to(scale, (resid.shape[0], half))
    input_ref[...] = low((resid - mean) * scale * gain + shift)


def start_copies(copies):
    for copy in copies:
        copy.start()
    for copy in copies:
        copy.wait()


def in_hbm(array):
    return pltpu.with_memory_space_constraint(array, pltpu.HBM)


def weight_pieces(upward, downward, layer, width, first):
    if first:
        return [(0, (layer,), upward), (1, (layer,), downward)]
    chunks = downward[1] // width
    pieces = [(0, (layer,), upward[2])]
    for at in range(chunks):
        pieces.append((1, (layer, slice(at * width, (at + 1) * width)), downward[2]))
    return pieces


def pack_copies(refs, out_ref, sems, pieces):
    copies = []
    at = 0
    for slot, (which, index, columns) in enumerate(pieces):
        copies.append(
            pltpu.make_async_copy(
                refs[which].at[index], out_ref.at[:, at : at + columns], sems.at[slot]
            )
        )
        at += columns
    return copies


def start_blocks(block_input, cotangent, joined, output, size):
    rows = block_input.shape[0] // size
    width = block_input.shape[1]
    pieces = weight_pieces(joined.shape[2], output.shape[2], 0, joined.shape[1], True)
    total = sum(piece[2] for piece in pieces)

    def kernel(input_ref, cotangent_ref, joined_ref, output_ref, *refs):
        outs, pack_ref, sems, pack_sems = refs[:size], *refs[size:]
        copies = []
        for step in range(size):
            here = slice(step * rows, (step + 1) * rows)
            copies.append(
                pltpu.make_async_copy(
                    input_ref.at[here], outs[step].at[:, :width], sems.at[2 * step]
                )
            )
            copies.append(
                pltpu.make_async_copy(
                    cotangent_ref.at[here], outs[step].at[:, width:], sems.at[2 * step + 1]
                )
            )
        copies += pack_copies((joined_ref, output_ref), pack_ref, pack_sems, pieces)
        start_copies(copies)

    outs = run(
        kernel,
        [in_hbm(array) for array in (block_input, cotangent, joined, output)],
        [shaped((rows, 2 * width), BF)] * size + [shaped((joined.shape[1], total), BF)],
        [pltpu.SemaphoreType.DMA((2 * size,)), pltpu.SemaphoreType.DMA((len(pieces),))],
        HBM,
    )
    return outs[:size], outs[size]


def start_vectors(vectors, biases):
    count, width = len(vectors), vectors[0].shape[1]

    def kernel(*refs):
        vector_refs = refs[:count]
        bias_refs = refs[count : count + len(biases)]
        out_ref = refs[count + len(biases)]
        bias_outs = refs[count + len(biases) + 1 : count + 2 * len(biases) + 1]
        landing = refs[count + 2 * len(biases) + 1 : -1]
        sems = refs[-1]
        pairs = list(zip(vector_refs, landing)) + list(zip(bias_refs, bias_outs))
        start_copies(
            [
                pltpu.make_async_copy(source, target, sems.at[at])
                for at, (source, target) in enumerate(pairs)
            ]
        )
        for at, ref in enumerate(landing):
            out_ref[LAYERS * at : LAYERS * (at + 1), :] = ref[...]

    outs = run(
        kernel,
        [in_hbm(array) for array in (*vectors, *biases)],
        [shaped((LAYERS * count, width), F32)] + [shaped(bias.shape, F32) for bias in biases],
        [pltpu.VMEM(vector.shape, F32) for vector in vectors]
        + [pltpu.SemaphoreType.DMA((count + len(biases),))],
        HBM,
    )
    return outs[0], outs[1:]


def turn_blocks(blocks, extra=0):
    size = len(blocks)
    rows = blocks[0].shape[0] - extra

    def kernel(*refs):
        block_refs, out_refs, turn = refs[:size], refs[size : 2 * size], refs[2 * size]
        shift = lax.axis_index(ROW) ^ lax.axis_index(COL)
        for at in range(size):
            turn[at] = block_refs[at][:rows, :]
        if extra:
            total = tree_sum([ref[rows:, :] for ref in block_refs])
        for at in range(size):
            out_refs[at][:rows, :] = turn[at ^ shift]
            if extra:
                out_refs[at][rows:, :] = total

    shape, dtype = blocks[0].shape, blocks[0].dtype
    return run(
        kernel,
        list(blocks),
        [shaped(shape, dtype)] * size,
        [pltpu.VMEM((size, rows, shape[1]), dtype)],
    )


def pack_weights(one, two, layer, width, first):
    last = two.shape[2] if first else two.shape
    pieces = weight_pieces(one.shape[2] if first else one.shape, last, layer, width, first)
    total = sum(piece[2] for piece in pieces)

    def kernel(one_ref, two_ref, out_ref, sems):
        start_copies(pack_copies((one_ref, two_ref), out_ref, sems, pieces))

    return pl.pallas_call(
        kernel,
        in_specs=[HBM] * 2,
        out_specs=VMEM,
        out_shape=shaped((width, total), BF),
        scratch_shapes=[pltpu.SemaphoreType.DMA((len(pieces),))],
        compiler_params=pltpu.CompilerParams(vmem_limit_bytes=VMEM_LIMIT),
    )(in_hbm(one), in_hbm(two))


def first_norm(got, vecs):
    size = len(got)
    rows, width = got[0].shape[0], got[0].shape[1] // 2

    def kernel(*refs):
        got_refs = refs[:size]
        vec_refs = refs[size : size + len(vecs)]
        resid_ref, cotangent_ref, input_ref, stats_ref = refs[size + len(vecs) :]
        whole = [ref[...] for ref in got_refs]
        resid = jnp.concatenate([wide(part[:, :width]) for part in whole], axis=1)
        cotangent_ref[...] = jnp.concatenate([part[:, width:] for part in whole], axis=1)
        resid_ref[...] = resid
        norm_into(
            resid,
            vector_row(vec_refs, GAIN_ONE * LAYERS),
            vector_row(vec_refs, SHIFT_ONE * LAYERS),
            input_ref,
            stats_ref,
        )

    full = size * width
    return run(
        kernel,
        [*got, *vecs],
        [
            shaped((rows, full), F32),
            shaped((rows, full), BF),
            shaped((rows, full), BF),
            shaped((rows, 256), F32),
        ],
    )


def next_norm(resid, parts, vecs, layer, bias_at, gain_at, shift_at):
    count = len(parts)
    next_layer = layer + 1 if gain_at == GAIN_ONE else layer

    def kernel(resid_ref, *refs):
        part_refs = refs[:count]
        vec_refs = refs[count : count + len(vecs)]
        out_ref, input_ref, stats_ref = refs[count + len(vecs) :]
        total = tree_sum([wide(ref[...]) for ref in part_refs])
        resid = resid_ref[...] + total + vector_row(vec_refs, bias_at * LAYERS + layer)
        out_ref[...] = resid
        norm_into(
            resid,
            vector_row(vec_refs, gain_at * LAYERS + next_layer),
            vector_row(vec_refs, shift_at * LAYERS + next_layer),
            input_ref,
            stats_ref,
        )

    rows, full = resid.shape
    return run(
        kernel,
        [resid, *parts, *vecs],
        [shaped((rows, full), F32), shaped((rows, full), BF), shaped((rows, 256), F32)],
    )


def cut_rows(value, refs):
    rows = refs[0].shape[0]
    for at, ref in enumerate(refs):
        ref[...] = value[at * rows : (at + 1) * rows]


def gathered(refs):
    return jnp.concatenate([ref[...] for ref in refs], axis=0)


def attention_forward(blocks, packs, query_bias, value_bias, layer):
    size, cols = len(blocks), len(packs)
    rows, full = blocks[0].shape
    length = size * rows
    width = full // cols
    across = query_bias.shape[1]
    heads = across // HD
    shift = int_log2(rows)
    steps = sends_of(cols)

    def kernel(*refs):
        block_refs = refs[:size]
        pack_refs = refs[size : size + cols]
        query_bias_ref, value_bias_ref = refs[size + cols : size + cols + 2]
        qkv_ref, probs_ref = refs[size + cols + 2 : size + cols + 4]
        part_refs = refs[size + cols + 4 : 2 * size + cols + 4]
        send_refs = refs[2 * size + cols + 4 :]
        mixed_ref = send_refs[0]
        full_first = gathered(block_refs)
        joined = tree_sum(
            [
                dot(full_first[:, at * width : (at + 1) * width], pack_refs[at][:, : 3 * across])
                for at in range(cols)
            ]
        )
        row = lax.axis_index(ROW)
        turn = row ^ lax.axis_index(COL)

        def where_is(axis):
            index = lax.broadcasted_iota(jnp.int32, (length, length), axis)
            return ((lax.shift_right_logical(index, shift) ^ turn) << shift) + (index & (rows - 1))

        offset = wide(where_is(1) - where_is(0))
        allowed = offset <= 0.0
        for head in range(heads):
            at = head * 3 * HD
            here = slice(head * HD, (head + 1) * HD)
            query = low(joined[:, at : at + HD] + query_bias_ref[layer : layer + 1, here])
            keys = low(joined[:, at + HD : at + 2 * HD])
            values = low(
                joined[:, at + 2 * HD : at + 3 * HD] + value_bias_ref[layer : layer + 1, here]
            )
            qkv_ref[:, at : at + HD] = query
            qkv_ref[:, at + HD : at + 2 * HD] = keys
            qkv_ref[:, at + 2 * HD : at + 3 * HD] = values
            index = jnp.full((1, length), row * heads + head + 1, jnp.int32)
            slope = jnp.exp2(wide(index) * (-8.0 / H))
            scores = dot_right(query, keys) * (1.0 / math.sqrt(HD)) + slope * offset
            scores = jnp.where(allowed, scores, masked_score)
            top = jnp.max(scores, axis=1, keepdims=True)
            log_total = top + jnp.log(jnp.sum(jnp.exp(scores - top), axis=1, keepdims=True))
            probs = jnp.exp(scores - log_total)
            probs_ref[head] = probs
            mixed_ref[:, here] = low(dot(low(probs), values))
        mixed = mixed_ref[:, :across]
        partial = jnp.concatenate(
            [low(dot(mixed, pack_ref[:, 3 * across : 3 * across + width])) for pack_ref in pack_refs],
            axis=1,
        )
        cut_rows(partial, part_refs)
        bundle_into(send_refs, steps, [mixed], [full_first], width)

    outs = run(
        kernel,
        [*blocks, *packs, query_bias, value_bias],
        [shaped((length, 3 * across), BF), shaped((heads, length, length), F32)]
        + [shaped((rows, full), BF)] * size
        + bundle_shapes(length, steps, across, 1, width),
    )
    return outs[:2], outs[2 : 2 + size], outs[2 + size :]


def bundle_into(refs, steps, shared, addressed, width):
    for at, ref in enumerate(refs):
        first = steps[at - 1] if at else 0
        count = first if at else 1
        column = 0
        for value in shared:
            ref[:, column : column + value.shape[1]] = value
            column += value.shape[1]
        for place in range(first, first + count):
            for value in addressed:
                ref[:, column : column + width] = value[:, place * width : (place + 1) * width]
                column += width


def bundle_shapes(length, steps, shared, addressed, width):
    counts = [1] + list(steps)
    return [shaped((length, shared + count * addressed * width), BF) for count in counts]


def feed_forward(blocks, packs, upward_bias, layer, middle=None, vecs=()):
    size, cols = len(blocks), len(packs)
    rows, full = blocks[0].shape
    length = size * rows
    width = full // cols
    units = upward_bias.shape[1]
    steps = sends_of(cols)
    extra = [middle, *vecs] if vecs else []
    parts = [shaped((length, width), BF)] * cols if vecs else [shaped((rows, full), BF)] * size

    def kernel(*refs):
        block_refs = refs[:size]
        pack_refs = refs[size : size + cols]
        bias_ref = refs[size + cols]
        more = refs[size + cols + 1 : size + cols + 1 + len(extra)]
        slope_ref = refs[size + cols + 1 + len(extra)]
        part_refs = refs[size + cols + 2 + len(extra) :][: len(parts)]
        send_refs = refs[size + cols + 2 + len(extra) + len(parts) :]
        full_second = gathered(block_refs)
        pre_act = tree_sum(
            [
                dot(full_second[:, at * width : (at + 1) * width], pack_refs[at][:, :units])
                for at in range(cols)
            ]
        )
        pre_act = pre_act + bias_ref[layer : layer + 1, :]
        inner = gelu_scale * (pre_act + gelu_coef * pre_act * pre_act * pre_act)
        tangent = jnp.tanh(inner)
        hidden = low(0.5 * pre_act * (1.0 + tangent))
        slope_ref[...] = 0.5 * (1.0 + tangent) + 0.5 * pre_act * (
            1.0 - tangent * tangent
        ) * gelu_scale * (1.0 + 3.0 * gelu_coef * pre_act * pre_act)
        partial = jnp.concatenate(
            [
                tree_sum(
                    [
                        dot(
                            hidden[:, at : at + width],
                            pack_ref[:, units + at : units + at + width],
                        )
                        for at in range(0, units, width)
                    ]
                )
                for pack_ref in pack_refs
            ],
            axis=1,
        )
        if vecs:
            bias = vector_row(more[1:], BIAS_DOWN * LAYERS + layer)
            shift = lax.axis_index(ROW) ^ lax.axis_index(COL)
            for step in range(size):
                block = partial[step * rows : (step + 1) * rows]
                if not step:
                    block = block + more[0][...] + bias
                at = pl.multiple_of((step ^ shift) * rows, rows)
                for place, ref in enumerate(part_refs):
                    ref[pl.ds(at, rows), :] = low(block[:, place * width : (place + 1) * width])
        else:
            cut_rows(low(partial), part_refs)
        bundle_into(send_refs, steps, [hidden], [full_second], width)

    outs = run(
        kernel,
        [*blocks, *packs, upward_bias, *extra],
        [shaped((length, units), F32)]
        + parts
        + bundle_shapes(length, steps, units, 1, width),
    )
    return outs[0], outs[1 : 1 + len(parts)], outs[1 + len(parts) :]


def feed_backward(blocks, packs, slope):
    size, cols = len(blocks), len(packs)
    rows, full = blocks[0].shape
    length = size * rows
    width = full // cols
    units = slope.shape[1]
    steps = sends_of(cols)

    def kernel(*refs):
        block_refs = refs[:size]
        pack_refs = refs[size : size + cols]
        slope_ref = refs[size + cols]
        part_refs = refs[size + cols + 1 : 2 * size + cols + 1]
        pre_ref = refs[2 * size + cols + 1]
        send_refs = refs[2 * size + cols + 2 :]
        full_grad = gathered(block_refs)
        grad_hidden = jnp.concatenate(
            [
                tree_sum(
                    [
                        dot_right(
                            full_grad[:, place * width : (place + 1) * width],
                            pack_refs[place][:, units + at : units + at + width],
                        )
                        for place in range(cols)
                    ]
                )
                for at in range(0, units, width)
            ],
            axis=1,
        )
        grad_pre = low(grad_hidden * slope_ref[...])
        pre_ref[...] = grad_pre
        partial = jnp.concatenate(
            [low(dot_right(grad_pre, pack_ref[:, :units])) for pack_ref in pack_refs], axis=1
        )
        cut_rows(partial, part_refs)
        bundle_into(send_refs, steps, [], [full_grad], width)

    outs = run(
        kernel,
        [*blocks, *packs, slope],
        [shaped((rows, full), BF)] * size
        + [shaped((length, units), BF)]
        + bundle_shapes(length, steps, 0, 1, width),
    )
    return outs[:size], outs[size], outs[size + 1 :]


def norm_back_math(grad_in, part_refs, resid_ref, stats_ref, gain):
    grad_out = tree_sum([wide(ref[...]) for ref in part_refs])
    half = stats_ref.shape[1] // 2
    scale = stats_ref[:, half : half + 1]
    normed = (resid_ref[...] - stats_ref[:, :1]) * scale
    grad_normed = grad_out * gain
    first = jnp.mean(grad_normed, axis=1, keepdims=True)
    second = jnp.mean(grad_normed * normed, axis=1, keepdims=True)
    total = grad_in + scale * (grad_normed - first - normed * second)
    sums = [
        jnp.sum(grad_out * normed, axis=0, keepdims=True),
        jnp.sum(grad_out, axis=0, keepdims=True),
    ]
    return total, sums


def norm_backward(grad_resid, parts, resid, stats, vecs, layer, gain_at, extra):
    count = len(parts)
    rows, full = grad_resid.shape

    def kernel(grad_ref, resid_ref, stats_ref, *refs):
        part_refs = refs[:count]
        vec_refs = refs[count : count + len(vecs)]
        out_ref, low_ref, sums_ref = refs[count + len(vecs) :]
        grad_in = wide(grad_ref[...])
        total, sums = norm_back_math(
            grad_in, part_refs, resid_ref, stats_ref, vector_row(vec_refs, gain_at * LAYERS + layer)
        )
        out_ref[...] = total
        low_ref[...] = low(total)
        if extra:
            sums.append(jnp.sum(total, axis=0, keepdims=True))
            sums.append(jnp.sum(grad_in, axis=0, keepdims=True))
        for at, value in enumerate(sums):
            sums_ref[at : at + 1, :] = value

    return run(
        kernel,
        [grad_resid, resid, stats, *parts, *vecs],
        [
            shaped((rows, full), F32),
            shaped((rows, full), BF),
            shaped((4 if extra else 2, full), F32),
        ],
    )


def last_backward(grad_resid, parts, resid, stats, vecs, other_sums, extra):
    count = len(parts)
    rows, full = grad_resid.shape
    cols = len(vecs)
    width = full // cols

    def kernel(grad_ref, resid_ref, stats_ref, *refs):
        part_refs = refs[:count]
        vec_refs = refs[count : count + cols]
        sums_refs = refs[count + cols : count + cols + len(other_sums)]
        out_refs = refs[count + cols + len(other_sums) :]
        total, sums = norm_back_math(
            grad_ref[...], part_refs, resid_ref, stats_ref, vector_row(vec_refs, GAIN_ONE * LAYERS)
        )
        lines = list(sums)
        for ref in sums_refs:
            lines += [ref[at : at + 1, :] for at in range(ref.shape[0])]
        for place in range(cols):
            here = slice(place * width, (place + 1) * width)
            out_refs[place][:rows, :] = total[:, here]
            out_refs[place][rows:, :] = jnp.zeros((extra, width), F32)
            for at, line in enumerate(lines):
                out_refs[place][rows + at : rows + at + 1, :] = line[:, here]

    return run(
        kernel,
        [grad_resid, resid, stats, *parts, *vecs, *other_sums],
        [shaped((rows + extra, width), F32)] * cols,
    )


def attention_backward(blocks, packs, qkv, probs, mixed, across):
    size, cols = len(blocks), len(packs)
    rows, full = blocks[0].shape
    length = size * rows
    width = full // cols
    heads = across // HD
    factor = 1.0 / math.sqrt(HD)

    def kernel(*refs):
        block_refs = refs[:size]
        pack_refs = refs[size : size + cols]
        qkv_ref, probs_ref, mixed_ref = refs[size + cols : size + cols + 3]
        part_refs = refs[size + cols + 3 : 2 * size + cols + 3]
        send_refs = refs[2 * size + cols + 3 :]
        joined_ref = send_refs[0]
        full_middle = gathered(block_refs)
        grad_mixed = low(
            tree_sum(
                [
                    dot_right(
                        full_middle[:, at * width : (at + 1) * width],
                        pack_refs[at][:, 3 * across : 3 * across + width],
                    )
                    for at in range(cols)
                ]
            )
        )
        for head in range(heads):
            at = head * 3 * HD
            here = slice(head * HD, (head + 1) * HD)
            query = qkv_ref[:, at : at + HD]
            keys = qkv_ref[:, at + HD : at + 2 * HD]
            values = qkv_ref[:, at + 2 * HD : at + 3 * HD]
            grad_here = grad_mixed[:, here]
            probs = probs_ref[head]
            value_sum = dot_left(low(probs), grad_here)
            grad_probs = dot_right(grad_here, values)
            delta = jnp.sum(wide(grad_here) * wide(mixed_ref[:, here]), axis=1, keepdims=True)
            grad_scores = low(probs * (grad_probs - delta))
            joined_ref[:, at : at + HD] = low(dot(grad_scores, keys) * factor)
            joined_ref[:, at + HD : at + 2 * HD] = low(dot_left(grad_scores, query) * factor)
            joined_ref[:, at + 2 * HD : at + 3 * HD] = low(value_sum)
        grad_joined = joined_ref[:, : 3 * across]
        partial = jnp.concatenate(
            [low(dot_right(grad_joined, pack_ref[:, : 3 * across])) for pack_ref in pack_refs],
            axis=1,
        )
        cut_rows(partial, part_refs)
        bundle_into(send_refs, sends_of(cols), [grad_joined], [full_middle], width)

    outs = run(
        kernel,
        [*blocks, *packs, qkv, probs, mixed],
        [shaped((rows, full), BF)] * size
        + bundle_shapes(length, sends_of(cols), 3 * across, 1, width),
    )
    return outs[:size], outs[size:]


def rows_of(refs, pick):
    return jnp.concatenate([ref[:, pick(at)] for at, ref in enumerate(refs)], axis=0)


def slices_of(refs, shared, width):
    def pick(place):
        start = shared + (place - high_bit(place) if place else 0) * width
        return slice(start, start + width)

    return rows_of(refs, pick)


def down_changes(ahead, grads, units, width):
    cols = len(ahead)

    def kernel(*refs):
        ahead_refs, grad_refs, out_ref = refs[:cols], refs[cols : 2 * cols], refs[2 * cols]
        grad_all = slices_of(grad_refs, 0, width)
        for at in range(0, units, width):
            hidden_all = rows_of(ahead_refs, lambda _: slice(at, at + width))
            out_ref[:, at : at + width] = low(dot_left(hidden_all, grad_all))

    return run(kernel, [*ahead, *grads], [shaped((width, units), BF)])[0]


def up_changes(ahead, pres, units, width):
    cols = len(ahead)

    def kernel(*refs):
        ahead_refs, pre_refs, out_ref = refs[:cols], refs[cols : 2 * cols], refs[2 * cols]
        pre_all = gathered(pre_refs)
        out_ref[:width, :] = low(dot_left(slices_of(ahead_refs, units, width), pre_all))
        total = jnp.sum(wide(pre_all), axis=0, keepdims=True)
        out_ref[width:, :] = low(jnp.broadcast_to(total, (16, units)))

    return run(kernel, [*ahead, *pres], [shaped((width + 16, units), BF)])[0]


def attention_changes(ahead, joined, across, width):
    cols = len(ahead)

    def kernel(*refs):
        ahead_refs, joined_refs, out_ref = refs[:cols], refs[cols : 2 * cols], refs[2 * cols]
        joined_all = rows_of(joined_refs, lambda _: slice(0, 3 * across))
        out_ref[:width, : 3 * across] = low(
            dot_left(slices_of(ahead_refs, across, width), joined_all)
        )
        total = jnp.sum(wide(joined_all), axis=0, keepdims=True)
        out_ref[width:, : 3 * across] = low(jnp.broadcast_to(total, (16, 3 * across)))
        mixed_all = rows_of(ahead_refs, lambda _: slice(0, across))
        change = low(dot_left(mixed_all, slices_of(joined_refs, 3 * across, width)))
        for at in range(0, across, width):
            column = 3 * across + at // width * width
            out_ref[:width, column : column + width] = change[at : at + width]
        out_ref[width:, 3 * across :] = jnp.zeros((16, out_ref.shape[1] - 3 * across), BF)

    return run(
        kernel,
        [*ahead, *joined],
        [shaped((width + 16, 4 * across), BF)],
    )[0]


def finish(own, other, layer, cuts, shapes, kept, line):
    width = own.shape[0] - (16 if line else 0)

    def kernel(own_ref, other_ref, *refs):
        out_refs = refs[len(kept or ()) :]
        for out_ref, pieces in zip(out_refs, cuts):
            row = 0
            for start, stop in pieces:
                out_ref[0, row : row + width, :] = wide(own_ref[:width, start:stop]) + wide(
                    other_ref[:width, start:stop]
                )
                row += width
        if line:
            out_refs[-1][...] = wide(own_ref[width : width + 8, :]) + wide(
                other_ref[width : width + 8, :]
            )

    def whole(array):
        return pl.BlockSpec(array.shape, lambda at: (0, 0))

    lines = [shaped((8, own.shape[1]), F32)] if line else []
    return pl.pallas_call(
        kernel,
        grid=(1,),
        in_specs=[whole(own), whole(other)] + [ANY] * len(kept or ()),
        out_specs=[pl.BlockSpec((1,) + shape[1:], lambda at: (layer, 0, 0)) for shape in shapes]
        + [whole(array) for array in lines],
        out_shape=[shaped(shape, F32) for shape in shapes] + lines,
        input_output_aliases={2 + at: at for at in range(len(kept or ()))},
        compiler_params=pltpu.CompilerParams(vmem_limit_bytes=VMEM_LIMIT),
    )(own, other, *(kept or ()))


def finish_vectors(own, other, up_lines, joined_lines, across):
    width = own.shape[1]
    units = up_lines[0].shape[1]
    heads = across // HD

    def kernel(*refs):
        own_ref, other_ref = refs[:2]
        up_refs = refs[2 : 2 + LAYERS]
        joined_refs = refs[2 + LAYERS : 2 + 2 * LAYERS]
        outs = refs[2 + 2 * LAYERS :]
        total = own_ref[...] + other_ref[...]
        for layer in range(LAYERS):
            here = slice(layer, layer + 1)
            for slot in range(6):
                outs[slot][here, :] = total[6 * layer + slot : 6 * layer + slot + 1, :]
            outs[6][here, :] = up_refs[layer][:1, :]
            for head in range(heads):
                at = head * 3 * HD
                there = slice(head * HD, (head + 1) * HD)
                outs[7][here, there] = joined_refs[layer][:1, at : at + HD]
                outs[8][here, there] = joined_refs[layer][:1, at + 2 * HD : at + 3 * HD]

    return run(
        kernel,
        [own, other, *up_lines, *joined_lines],
        [shaped((LAYERS, width), F32)] * 6
        + [shaped((LAYERS, units), F32)]
        + [shaped((LAYERS, across), F32)] * 2,
    )


def end_place(got, extra=0):
    size = len(got)
    rows, width = got[0].shape[0] - extra, got[0].shape[1]

    def kernel(*refs):
        for at in range(size):
            refs[size][at * rows : (at + 1) * rows, :] = refs[at][:rows, :]
        if extra:
            refs[size + 1][...] = tree_sum([ref[rows:, :] for ref in refs[:size]])

    outs = [shaped((rows * size, width), got[0].dtype)]
    if extra:
        outs.append(shaped((extra, width), got[0].dtype))
    return run(kernel, list(got), outs)


def turn_in(blocks):
    got = turn_blocks(trade(blocks, ROW))
    return trade(got, COL)


def turn_out(blocks, extra=0):
    got = turn_blocks(trade(blocks, COL), extra)
    return end_place(trade(got, ROW), extra)


def turn_sum(blocks):
    got = turn_blocks(trade(blocks, COL))
    return sum_blocks(trade(got, ROW))


def sum_blocks(got):
    def kernel(*refs):
        refs[-1][...] = low(tree_sum([wide(ref[...]) for ref in refs[:-1]]))

    return run(kernel, list(got), [shaped(got[0].shape, BF)])[0]


def shards(
    block_input,
    cotangent,
    first_gain,
    first_shift,
    joined_weight,
    query_bias,
    value_bias,
    output_weight,
    output_bias,
    second_gain,
    second_shift,
    upward_weight,
    upward_bias,
    downward_weight,
    downward_bias,
):
    across = query_bias.shape[1]
    units = upward_bias.shape[1]
    width = block_input.shape[1]
    size, cols = lax.axis_size(ROW), lax.axis_size(COL)
    steps = sends_of(cols)
    extra = -(-6 * LAYERS // 8) * 8

    def exchange(sends):
        return [sends[0]] + relay(dict(zip(steps, sends[1:])), COL)

    blocks, first_pack = start_blocks(block_input, cotangent, joined_weight, output_weight, size)
    vectors, (query_bias, value_bias, upward_bias) = start_vectors(
        [first_gain, first_shift, output_bias, second_gain, second_shift, downward_bias],
        [query_bias, value_bias, upward_bias],
    )
    got = turn_in(blocks)
    vecs = relay_all(vectors, COL)
    weights = []
    for layer in range(LAYERS):
        weights.append([])
        for first in (True, False):
            if layer or not first:
                pair = (joined_weight, output_weight) if first else (upward_weight, downward_weight)
                pack = pack_weights(*pair, layer, width, first)
            else:
                pack = first_pack
            weights[layer].append(relay_all(pack, COL))
    resid, grad_resid, norm_input, stats = first_norm(got, vecs)
    saved = []
    for layer in range(LAYERS):
        attention_packs, feed_packs = weights[layer]
        first_kept = (resid, stats)
        (qkv, probs), parts, sends = attention_forward(
            spread(norm_input, ROW), attention_packs, query_bias, value_bias, layer
        )
        attention_ahead = exchange(sends)
        middle, norm_input, stats = next_norm(
            resid, trade(parts, ROW), vecs, layer, BIAS_OUT, GAIN_TWO, SHIFT_TWO
        )
        second_kept = (middle, stats)
        slope, parts, sends = feed_forward(
            spread(norm_input, ROW),
            feed_packs,
            upward_bias,
            layer,
            *((middle, vecs) if layer + 1 == LAYERS else ()),
        )
        feed_ahead = exchange(sends)
        saved.append((first_kept, second_kept, qkv, probs, slope, attention_ahead, feed_ahead))
        if layer + 1 < LAYERS:
            resid, norm_input, stats = next_norm(
                middle, trade(parts, ROW), vecs, layer, BIAS_DOWN, GAIN_ONE, SHIFT_ONE
            )
        else:
            block_output = turn_sum(parts)

    grad_low = grad_resid
    sums = []
    down_outs = up_outs = attention_outs = None
    up_lines, joined_lines = [None] * LAYERS, [None] * LAYERS
    for layer in reversed(range(LAYERS)):
        attention_packs, feed_packs = weights[layer]
        first_kept, second_kept, qkv, probs, slope, attention_ahead, feed_ahead = saved[layer]
        parts, grad_pre, sends = feed_backward(spread(grad_low, ROW), feed_packs, slope)
        grads = exchange(sends)
        pres = relay_all(grad_pre, COL)
        grad_middle, middle_low, second_sums = norm_backward(
            grad_resid, trade(parts, ROW), *second_kept, vecs, layer, GAIN_TWO, True
        )
        parts, sends = attention_backward(
            spread(middle_low, ROW), attention_packs, qkv, probs, attention_ahead[0], across
        )
        joined = exchange(sends)
        parts = trade(parts, ROW)
        if layer:
            grad_resid, grad_low, first_sums = norm_backward(
                grad_middle, parts, *first_kept, vecs, layer, GAIN_ONE, False
            )
            sums = [first_sums, second_sums] + sums
        else:
            blocks = last_backward(
                grad_middle, parts, *first_kept, vecs, [second_sums] + sums, extra
            )
        change = down_changes(feed_ahead, grads, units, width)
        down_outs = finish(
            change,
            axis_swap(change, DP, 1),
            layer,
            [[(at, at + width) for at in range(0, units, width)]],
            [downward_weight.shape],
            down_outs,
            False,
        )
        change = up_changes(feed_ahead, pres, units, width)
        *up_outs, up_lines[layer] = finish(
            change,
            axis_swap(change, DP, 1),
            layer,
            [[(0, units)]],
            [upward_weight.shape],
            up_outs,
            True,
        )
        change = attention_changes(attention_ahead, joined, across, width)
        chunk = range(3 * across, 3 * across + across // width * width, width)
        *attention_outs, joined_lines[layer] = finish(
            change,
            axis_swap(change, DP, 1),
            layer,
            [[(0, 3 * across)], [(at, at + width) for at in chunk]],
            [joined_weight.shape, output_weight.shape],
            attention_outs,
            True,
        )
    input_gradient, totals = turn_out(blocks, extra)
    vector_sums = finish_vectors(totals, axis_swap(totals, DP, 1), up_lines, joined_lines, across)
    return (
        block_output,
        input_gradient,
        vector_sums[0],
        vector_sums[1],
        attention_outs[0],
        vector_sums[7],
        vector_sums[8],
        attention_outs[1],
        vector_sums[4],
        vector_sums[2],
        vector_sums[3],
        up_outs[0],
        vector_sums[6],
        down_outs[0],
        vector_sums[5],
    )


def solution(mesh):
    return jax.shard_map(
        shards,
        mesh=mesh,
        in_specs=(
            P((DP, ROW), COL),
            P((DP, ROW), COL),
            P(None, COL),
            P(None, COL),
            P(None, COL, ROW),
            P(None, ROW),
            P(None, ROW),
            P(None, ROW, COL),
            P(None, COL),
            P(None, COL),
            P(None, COL),
            P(None, COL, ROW),
            P(None, ROW),
            P(None, ROW, COL),
            P(None, COL),
        ),
        out_specs=(
            P((DP, ROW), COL),
            P((DP, ROW), COL),
            P(None, COL),
            P(None, COL),
            P(None, COL, ROW),
            P(None, ROW),
            P(None, ROW),
            P(None, ROW, COL),
            P(None, COL),
            P(None, COL),
            P(None, COL),
            P(None, COL, ROW),
            P(None, ROW),
            P(None, ROW, COL),
            P(None, COL),
        ),
        check_vma=False,
    )
```

```python
import math

import jax
import jax.numpy as jnp
from jax import lax
from jax.experimental import pallas as pl
from jax.experimental.pallas import tpu as pltpu
from jax.sharding import PartitionSpec as P


H = 16
HD = 64
LAYERS = 2

VMEM_LIMIT = 16 * 1024 * 1024
DP, ROW, COL = "dp", "row", "col"
GAIN_ONE, SHIFT_ONE, BIAS_OUT, GAIN_TWO, SHIFT_TWO, BIAS_DOWN = range(6)

norm_epsilon = 1e-05
gelu_coef = 0.044715
gelu_scale = math.sqrt(2.0 / math.pi)
masked_score = -1e30


def int_log2(value):
    return value.bit_length() - 1


def axis_swap(local, axis, step):
    size = lax.axis_size(axis)
    return lax.ppermute(local, axis, [(place, place ^ step) for place in range(size)])


def spread(local, axis):
    size = lax.axis_size(axis)
    return [local] + [axis_swap(local, axis, step) for step in range(1, size)]


def trade(blocks, axis):
    return [blocks[0]] + [axis_swap(blocks[step], axis, step) for step in range(1, len(blocks))]


def relay(sends, axis):
    size = lax.axis_size(axis)
    got = {}
    step = size // 2
    while step:
        arrived = {place ^ step: axis_swap(got[place], axis, step) for place in sorted(got)}
        arrived[step] = axis_swap(sends[step], axis, step)
        got.update(arrived)
        step //= 2
    return [got[place] for place in range(1, size)]


def sends_of(size):
    steps = []
    step = 1
    while step < size:
        steps.append(step)
        step *= 2
    return steps


def relay_all(local, axis):
    return [local] + relay({step: local for step in sends_of(lax.axis_size(axis))}, axis)


def high_bit(place):
    return 1 << int_log2(place)


def tree_sum(parts):
    parts = list(parts)
    while len(parts) > 1:
        parts = [parts[at] + parts[at + 1] for at in range(0, len(parts), 2)]
    return parts[0]


def dot(left, right):
    return lax.dot_general(left, right, (((1,), (0,)), ((), ())), preferred_element_type=jnp.float32)


def dot_right(left, right):
    return lax.dot_general(left, right, (((1,), (1,)), ((), ())), preferred_element_type=jnp.float32)


def dot_left(left, right):
    return lax.dot_general(left, right, (((0,), (0,)), ((), ())), preferred_element_type=jnp.float32)


def low(values):
    return values.astype(jnp.bfloat16)


def wide(values):
    return values.astype(jnp.float32)


def shaped(shape, dtype):
    return jax.ShapeDtypeStruct(shape, dtype)


BF = jnp.bfloat16
F32 = jnp.float32


VMEM = pl.BlockSpec(memory_space=pltpu.VMEM)
ANY = pl.BlockSpec(memory_space=pl.ANY)
HBM = pl.BlockSpec(memory_space=pltpu.HBM)


def run(kernel, arrays, outs, scratch=(), spec=None):
    return pl.pallas_call(
        kernel,
        in_specs=[spec or VMEM] * len(arrays),
        out_specs=[VMEM] * len(outs),
        out_shape=outs,
        scratch_shapes=list(scratch),
        compiler_params=pltpu.CompilerParams(vmem_limit_bytes=VMEM_LIMIT),
    )(*arrays)


def vector_row(vecs, at):
    return jnp.concatenate([vec[at : at + 1, :] for vec in vecs], axis=1)


def norm_into(resid, gain, shift, input_ref, stats_ref):
    mean = jnp.mean(resid, axis=1, keepdims=True)
    spread_out = jnp.mean(resid * resid, axis=1, keepdims=True) - mean * mean
    scale = lax.rsqrt(spread_out + norm_epsilon)
    half = stats_ref.shape[1] // 2
    stats_ref[:, :half] = jnp.broadcast_to(mean, (resid.shape[0], half))
    stats_ref[:, half:] = jnp.broadcast_to(scale, (resid.shape[0], half))
    input_ref[...] = low((resid - mean) * scale * gain + shift)


def start_copies(copies):
    for copy in copies:
        copy.start()
    for copy in copies:
        copy.wait()


def in_hbm(array):
    return pltpu.with_memory_space_constraint(array, pltpu.HBM)


def weight_pieces(upward, downward, layer, width, first):
    if first:
        return [(0, (layer,), upward), (1, (layer,), downward)]
    chunks = downward[1] // width
    pieces = [(0, (layer,), upward[2])]
    for at in range(chunks):
        pieces.append((1, (layer, slice(at * width, (at + 1) * width)), downward[2]))
    return pieces


def pack_copies(refs, out_ref, sems, pieces):
    copies = []
    at = 0
    for slot, (which, index, columns) in enumerate(pieces):
        copies.append(
            pltpu.make_async_copy(
                refs[which].at[index], out_ref.at[:, at : at + columns], sems.at[slot]
            )
        )
        at += columns
    return copies


def start_vectors(vectors, biases):
    count, width = len(vectors), vectors[0].shape[1]

    def kernel(*refs):
        vector_refs = refs[:count]
        bias_refs = refs[count : count + len(biases)]
        out_ref = refs[count + len(biases)]
        bias_outs = refs[count + len(biases) + 1 : count + 2 * len(biases) + 1]
        landing = refs[count + 2 * len(biases) + 1 : -1]
        sems = refs[-1]
        pairs = list(zip(vector_refs, landing)) + list(zip(bias_refs, bias_outs))
        start_copies(
            [
                pltpu.make_async_copy(source, target, sems.at[at])
                for at, (source, target) in enumerate(pairs)
            ]
        )
        for at, ref in enumerate(landing):
            out_ref[LAYERS * at : LAYERS * (at + 1), :] = ref[...]

    outs = run(
        kernel,
        [in_hbm(array) for array in (*vectors, *biases)],
        [shaped((LAYERS * count, width), F32)] + [shaped(bias.shape, F32) for bias in biases],
        [pltpu.VMEM(vector.shape, F32) for vector in vectors]
        + [pltpu.SemaphoreType.DMA((count + len(biases),))],
        HBM,
    )
    return outs[0], outs[1:]


def turn_blocks(blocks, extra=0):
    size = len(blocks)
    rows = blocks[0].shape[0] - extra

    def kernel(*refs):
        block_refs, out_refs, turn = refs[:size], refs[size : 2 * size], refs[2 * size]
        shift = lax.axis_index(ROW) ^ lax.axis_index(COL)
        for at in range(size):
            turn[at] = block_refs[at][:rows, :]
        if extra:
            total = tree_sum([wide(ref[rows:, :]) for ref in block_refs])
        for at in range(size):
            out_refs[at][:rows, :] = turn[at ^ shift]
            if extra:
                out_refs[at][rows:, :] = total.astype(out_refs[at].dtype)

    shape, dtype = blocks[0].shape, blocks[0].dtype
    return run(
        kernel,
        list(blocks),
        [shaped(shape, dtype)] * size,
        [pltpu.VMEM((size, rows, shape[1]), dtype)],
    )


def pack_weights(one, two, layer, width, first):
    last = two.shape[2] if first else two.shape
    pieces = weight_pieces(one.shape[2] if first else one.shape, last, layer, width, first)
    total = sum(piece[2] for piece in pieces)

    def kernel(one_ref, two_ref, out_ref, sems):
        start_copies(pack_copies((one_ref, two_ref), out_ref, sems, pieces))

    return pl.pallas_call(
        kernel,
        in_specs=[HBM] * 2,
        out_specs=VMEM,
        out_shape=shaped((width, total), BF),
        scratch_shapes=[pltpu.SemaphoreType.DMA((len(pieces),))],
        compiler_params=pltpu.CompilerParams(vmem_limit_bytes=VMEM_LIMIT),
    )(in_hbm(one), in_hbm(two))


def own_rows(blocks, step, rows):
    at = pl.multiple_of((lax.axis_index(ROW) ^ step) * rows, rows)
    return jnp.concatenate([ref[pl.ds(at, rows), :] for ref in blocks], axis=1)


def first_norm(got, vecs, size):
    cols = len(got)
    length, width = got[0].shape
    rows, full = length // size, width * cols

    def kernel(*refs):
        got_refs = refs[:cols]
        vec_refs = refs[cols : 2 * cols]
        resid_ref, normed_ref, scale_ref = refs[2 * cols : 2 * cols + 3]
        input_refs = refs[2 * cols + 3 :]
        gain = vector_row(vec_refs, GAIN_ONE * LAYERS)
        shift = vector_row(vec_refs, SHIFT_ONE * LAYERS)
        for step in range(size):
            here = slice(step * rows, (step + 1) * rows)
            resid = wide(own_rows(got_refs, step, rows))
            if not step:
                resid_ref[...] = resid
            mean = jnp.mean(resid, axis=1, keepdims=True)
            spread_out = jnp.mean(resid * resid, axis=1, keepdims=True) - mean * mean
            scale = lax.rsqrt(spread_out + norm_epsilon)
            normed = (resid - mean) * scale
            normed_ref[here, :] = normed
            scale_ref[here, :] = jnp.broadcast_to(scale, (rows, 128))
            input_refs[step][...] = low(normed * gain + shift)

    outs = run(
        kernel,
        [*got, *vecs],
        [shaped((rows, full), F32), shaped((length, full), F32), shaped((length, 128), F32)]
        + [shaped((rows, full), BF)] * size,
    )
    return outs[0], (outs[1], outs[2]), outs[3:]


def row_blocks(got, size):
    length, width = got[0].shape
    rows = length // size

    def kernel(*refs):
        for step in range(size):
            refs[len(got) + step][...] = own_rows(refs[: len(got)], step, rows)

    return run(kernel, list(got), [shaped((rows, width * len(got)), BF)] * size)


def next_norm(resid, parts, vecs, layer, bias_at, gain_at, shift_at):
    count = len(parts)
    next_layer = layer + 1 if gain_at == GAIN_ONE else layer

    def kernel(resid_ref, *refs):
        part_refs = refs[:count]
        vec_refs = refs[count : count + len(vecs)]
        out_ref, input_ref, stats_ref = refs[count + len(vecs) :]
        total = tree_sum([wide(ref[...]) for ref in part_refs])
        resid = resid_ref[...] + total + vector_row(vec_refs, bias_at * LAYERS + layer)
        out_ref[...] = resid
        norm_into(
            resid,
            vector_row(vec_refs, gain_at * LAYERS + next_layer),
            vector_row(vec_refs, shift_at * LAYERS + next_layer),
            input_ref,
            stats_ref,
        )

    rows, full = resid.shape
    return run(
        kernel,
        [resid, *parts, *vecs],
        [shaped((rows, full), F32), shaped((rows, full), BF), shaped((rows, 256), F32)],
    )


def cut_rows(value, refs):
    rows = refs[0].shape[0]
    for at, ref in enumerate(refs):
        ref[...] = value[at * rows : (at + 1) * rows]


def cut_turned(partial, ours, refs):
    rows, width = ours.shape[0], refs[0].shape[1]
    for step in range(partial.shape[0] // rows):
        block = partial[step * rows : (step + 1) * rows]
        if not step:
            block = block + ours
        at = pl.multiple_of((lax.axis_index(ROW) ^ step) * rows, rows)
        for place, ref in enumerate(refs):
            ref[pl.ds(at, rows), :] = low(block[:, place * width : (place + 1) * width])


def gathered(refs):
    return jnp.concatenate([ref[...] for ref in refs], axis=0)


def attention_forward(blocks, packs, query_bias, value_bias, layer):
    size, cols = len(blocks), len(packs)
    rows, full = blocks[0].shape
    length = size * rows
    width = full // cols
    across = query_bias.shape[1]
    heads = across // HD
    shift = int_log2(rows)
    steps = sends_of(cols)

    def kernel(*refs):
        block_refs = refs[:size]
        pack_refs = refs[size : size + cols]
        query_bias_ref, value_bias_ref = refs[size + cols : size + cols + 2]
        qkv_ref, probs_ref = refs[size + cols + 2 : size + cols + 4]
        part_refs = refs[size + cols + 4 : 2 * size + cols + 4]
        send_refs = refs[2 * size + cols + 4 :]
        mixed_ref = send_refs[0]
        full_first = gathered(block_refs)
        joined = tree_sum(
            [
                dot(full_first[:, at * width : (at + 1) * width], pack_refs[at][:, : 3 * across])
                for at in range(cols)
            ]
        )
        row = lax.axis_index(ROW)

        def where_is(axis):
            index = lax.broadcasted_iota(jnp.int32, (length, length), axis)
            return ((lax.shift_right_logical(index, shift) ^ row) << shift) + (index & (rows - 1))

        offset = wide(where_is(1) - where_is(0))
        allowed = offset <= 0.0
        for head in range(heads):
            at = head * 3 * HD
            here = slice(head * HD, (head + 1) * HD)
            query = low(joined[:, at : at + HD] + query_bias_ref[layer : layer + 1, here])
            keys = low(joined[:, at + HD : at + 2 * HD])
            values = low(
                joined[:, at + 2 * HD : at + 3 * HD] + value_bias_ref[layer : layer + 1, here]
            )
            qkv_ref[:, at : at + HD] = query
            qkv_ref[:, at + HD : at + 2 * HD] = keys
            qkv_ref[:, at + 2 * HD : at + 3 * HD] = values
            index = jnp.full((1, length), row * heads + head + 1, jnp.int32)
            slope = jnp.exp2(wide(index) * (-8.0 / H))
            scores = dot_right(query, keys) * (1.0 / math.sqrt(HD)) + slope * offset
            scores = jnp.where(allowed, scores, masked_score)
            top = jnp.max(scores, axis=1, keepdims=True)
            log_total = top + jnp.log(jnp.sum(jnp.exp(scores - top), axis=1, keepdims=True))
            probs = jnp.exp(scores - log_total)
            probs_ref[head] = probs
            mixed_ref[:, here] = low(dot(low(probs), values))
        mixed = mixed_ref[:, :across]
        partial = jnp.concatenate(
            [low(dot(mixed, pack_ref[:, 3 * across : 3 * across + width])) for pack_ref in pack_refs],
            axis=1,
        )
        cut_rows(partial, part_refs)
        bundle_into(send_refs, steps, [mixed], [full_first], width)

    outs = run(
        kernel,
        [*blocks, *packs, query_bias, value_bias],
        [shaped((length, 3 * across), BF), shaped((heads, length, length), F32)]
        + [shaped((rows, full), BF)] * size
        + bundle_shapes(length, steps, across, 1, width),
    )
    return outs[:2], outs[2 : 2 + size], outs[2 + size :]


def bundle_into(refs, steps, shared, addressed, width):
    for at, ref in enumerate(refs):
        first = steps[at - 1] if at else 0
        count = first if at else 1
        column = 0
        for value in shared:
            ref[:, column : column + value.shape[1]] = value
            column += value.shape[1]
        for place in range(first, first + count):
            for value in addressed:
                ref[:, column : column + width] = value[:, place * width : (place + 1) * width]
                column += width


def bundle_shapes(length, steps, shared, addressed, width):
    counts = [1] + list(steps)
    return [shaped((length, shared + count * addressed * width), BF) for count in counts]


def feed_forward(blocks, packs, upward_bias, layer, middle=None, vecs=()):
    size, cols = len(blocks), len(packs)
    rows, full = blocks[0].shape
    length = size * rows
    width = full // cols
    units = upward_bias.shape[1]
    steps = sends_of(cols)
    extra = [middle, *vecs] if vecs else []
    parts = [shaped((length, width), BF)] * cols if vecs else [shaped((rows, full), BF)] * size

    def kernel(*refs):
        block_refs = refs[:size]
        pack_refs = refs[size : size + cols]
        bias_ref = refs[size + cols]
        more = refs[size + cols + 1 : size + cols + 1 + len(extra)]
        slope_ref = refs[size + cols + 1 + len(extra)]
        part_refs = refs[size + cols + 2 + len(extra) :][: len(parts)]
        send_refs = refs[size + cols + 2 + len(extra) + len(parts) :]
        full_second = gathered(block_refs)
        pre_act = tree_sum(
            [
                dot(full_second[:, at * width : (at + 1) * width], pack_refs[at][:, :units])
                for at in range(cols)
            ]
        )
        pre_act = pre_act + bias_ref[layer : layer + 1, :]
        inner = gelu_scale * (pre_act + gelu_coef * pre_act * pre_act * pre_act)
        tangent = jnp.tanh(inner)
        hidden = low(0.5 * pre_act * (1.0 + tangent))
        slope_ref[...] = 0.5 * (1.0 + tangent) + 0.5 * pre_act * (
            1.0 - tangent * tangent
        ) * gelu_scale * (1.0 + 3.0 * gelu_coef * pre_act * pre_act)
        partial = jnp.concatenate(
            [
                tree_sum(
                    [
                        dot(
                            hidden[:, at : at + width],
                            pack_ref[:, units + at : units + at + width],
                        )
                        for at in range(0, units, width)
                    ]
                )
                for pack_ref in pack_refs
            ],
            axis=1,
        )
        if vecs:
            bias = vector_row(more[1:], BIAS_DOWN * LAYERS + layer)
            cut_turned(partial, more[0][...] + bias, part_refs)
        else:
            cut_rows(low(partial), part_refs)
        bundle_into(send_refs, steps, [hidden], [full_second], width)

    outs = run(
        kernel,
        [*blocks, *packs, upward_bias, *extra],
        [shaped((length, units), F32)]
        + parts
        + bundle_shapes(length, steps, units, 1, width),
    )
    return outs[0], outs[1 : 1 + len(parts)], outs[1 + len(parts) :]


def feed_backward(blocks, packs, slope):
    size, cols = len(blocks), len(packs)
    rows, full = blocks[0].shape
    length = size * rows
    width = full // cols
    units = slope.shape[1]
    steps = sends_of(cols)

    def kernel(*refs):
        block_refs = refs[:size]
        pack_refs = refs[size : size + cols]
        slope_ref = refs[size + cols]
        part_refs = refs[size + cols + 1 : 2 * size + cols + 1]
        pre_ref = refs[2 * size + cols + 1]
        send_refs = refs[2 * size + cols + 2 :]
        full_grad = gathered(block_refs)
        grad_hidden = jnp.concatenate(
            [
                tree_sum(
                    [
                        dot_right(
                            full_grad[:, place * width : (place + 1) * width],
                            pack_refs[place][:, units + at : units + at + width],
                        )
                        for place in range(cols)
                    ]
                )
                for at in range(0, units, width)
            ],
            axis=1,
        )
        grad_pre = low(grad_hidden * slope_ref[...])
        pre_ref[...] = grad_pre
        partial = jnp.concatenate(
            [low(dot_right(grad_pre, pack_ref[:, :units])) for pack_ref in pack_refs], axis=1
        )
        cut_rows(partial, part_refs)
        bundle_into(send_refs, steps, [], [full_grad], width)

    outs = run(
        kernel,
        [*blocks, *packs, slope],
        [shaped((rows, full), BF)] * size
        + [shaped((length, units), BF)]
        + bundle_shapes(length, steps, 0, 1, width),
    )
    return outs[:size], outs[size], outs[size + 1 :]


def bundle_blocks(blocks, cols):
    rows, full = blocks[0].shape
    width = full // cols
    steps = sends_of(cols)

    def kernel(*refs):
        bundle_into(refs[len(blocks) :], steps, [], [gathered(refs[: len(blocks)])], width)

    return run(kernel, list(blocks), bundle_shapes(len(blocks) * rows, steps, 0, 1, width))


def norm_back_math(grad_in, part_refs, resid_ref, stats_ref, gain):
    grad_out = tree_sum([wide(ref[...]) for ref in part_refs])
    half = stats_ref.shape[1] // 2
    scale = stats_ref[:, half : half + 1]
    normed = (resid_ref[...] - stats_ref[:, :1]) * scale
    grad_normed = grad_out * gain
    first = jnp.mean(grad_normed, axis=1, keepdims=True)
    second = jnp.mean(grad_normed * normed, axis=1, keepdims=True)
    total = grad_in + scale * (grad_normed - first - normed * second)
    sums = [
        jnp.sum(grad_out * normed, axis=0, keepdims=True),
        jnp.sum(grad_out, axis=0, keepdims=True),
    ]
    return total, sums


def norm_backward(grad_resid, parts, resid, stats, vecs, layer, gain_at, extra):
    count = len(parts)
    rows, full = grad_resid.shape

    def kernel(grad_ref, resid_ref, stats_ref, *refs):
        part_refs = refs[:count]
        vec_refs = refs[count : count + len(vecs)]
        out_ref, low_ref, sums_ref = refs[count + len(vecs) :]
        grad_in = wide(grad_ref[...])
        total, sums = norm_back_math(
            grad_in, part_refs, resid_ref, stats_ref, vector_row(vec_refs, gain_at * LAYERS + layer)
        )
        out_ref[...] = total
        low_ref[...] = low(total)
        if extra:
            sums.append(jnp.sum(total, axis=0, keepdims=True))
            sums.append(jnp.sum(grad_in, axis=0, keepdims=True))
        for at, value in enumerate(sums):
            sums_ref[at : at + 1, :] = value

    return run(
        kernel,
        [grad_resid, resid, stats, *parts, *vecs],
        [
            shaped((rows, full), F32),
            shaped((rows, full), BF),
            shaped((4 if extra else 2, full), F32),
        ],
    )


def attention_backward(blocks, packs, qkv, probs, mixed, across, last=None):
    size, cols = len(blocks), len(packs)
    rows, full = blocks[0].shape
    length = size * rows
    width = full // cols
    heads = across // HD
    factor = 1.0 / math.sqrt(HD)

    extra = []
    parts = [shaped((rows, full), BF)] * size
    sends = bundle_shapes(length, sends_of(cols), 3 * across, 1, width)
    if last:
        sends = [shaped((length, 3 * across), BF)]
        kept, grad_middle, vecs, other_sums = last
        extra = [*kept, grad_middle, *vecs, *other_sums]
        parts = [shaped((length + 16, width), BF)] * cols

    def kernel(*refs):
        block_refs = refs[:size]
        pack_refs = refs[size : size + cols]
        qkv_ref, probs_ref, mixed_ref = refs[size + cols : size + cols + 3]
        more = refs[size + cols + 3 : size + cols + 3 + len(extra)]
        part_refs = refs[size + cols + 3 + len(extra) :][: len(parts)]
        send_refs = refs[size + cols + 3 + len(extra) + len(parts) :]
        joined_ref = send_refs[0]
        full_middle = gathered(block_refs)
        grad_mixed = low(
            tree_sum(
                [
                    dot_right(
                        full_middle[:, at * width : (at + 1) * width],
                        pack_refs[at][:, 3 * across : 3 * across + width],
                    )
                    for at in range(cols)
                ]
            )
        )
        for head in range(heads):
            at = head * 3 * HD
            here = slice(head * HD, (head + 1) * HD)
            query = qkv_ref[:, at : at + HD]
            keys = qkv_ref[:, at + HD : at + 2 * HD]
            values = qkv_ref[:, at + 2 * HD : at + 3 * HD]
            grad_here = grad_mixed[:, here]
            probs = probs_ref[head]
            value_sum = dot_left(low(probs), grad_here)
            grad_probs = dot_right(grad_here, values)
            delta = jnp.sum(wide(grad_here) * wide(mixed_ref[:, here]), axis=1, keepdims=True)
            grad_scores = low(probs * (grad_probs - delta))
            joined_ref[:, at : at + HD] = low(dot(grad_scores, keys) * factor)
            joined_ref[:, at + HD : at + 2 * HD] = low(dot_left(grad_scores, query) * factor)
            joined_ref[:, at + 2 * HD : at + 3 * HD] = low(value_sum)
        grad_joined = joined_ref[:, : 3 * across]
        partial = jnp.concatenate(
            [dot_right(grad_joined, pack_ref[:, : 3 * across]) for pack_ref in pack_refs],
            axis=1,
        )
        if last:
            normed, scale = more[0][...], more[1][:, :1]
            grad_normed = partial * vector_row(more[3 : 3 + cols], GAIN_ONE * LAYERS)
            first = jnp.mean(grad_normed, axis=1, keepdims=True)
            second = jnp.mean(grad_normed * normed, axis=1, keepdims=True)
            cut_turned(
                scale * (grad_normed - first - normed * second), more[2][...], part_refs
            )
            lines = [
                jnp.sum(partial * normed, axis=0, keepdims=True),
                jnp.sum(partial, axis=0, keepdims=True),
            ]
            for ref in more[3 + cols :]:
                lines += [ref[at : at + 1, :] for at in range(ref.shape[0])]
            lines.append(jnp.zeros((16 - len(lines), full), F32))
            lines = low(jnp.concatenate(lines, axis=0))
            for place, ref in enumerate(part_refs):
                ref[length:, :] = lines[:, place * width : (place + 1) * width]
        else:
            cut_rows(low(partial), part_refs)
        if not last:
            bundle_into(send_refs, sends_of(cols), [grad_joined], [full_middle], width)

    outs = run(
        kernel,
        [*blocks, *packs, qkv, probs, mixed, *extra],
        parts + sends,
    )
    return outs[: len(parts)], outs[len(parts) :]


def rows_of(refs, pick):
    return jnp.concatenate([ref[:, pick(at)] for at, ref in enumerate(refs)], axis=0)


def slices_of(refs, shared, width):
    def pick(place):
        start = shared + (place - high_bit(place) if place else 0) * width
        return slice(start, start + width)

    return rows_of(refs, pick)


def down_changes(ahead, grads, units, width):
    cols = len(ahead)

    def kernel(*refs):
        ahead_refs, grad_refs, out_ref = refs[:cols], refs[cols : 2 * cols], refs[2 * cols]
        grad_all = slices_of(grad_refs, 0, width)
        for at in range(0, units, width):
            hidden_all = rows_of(ahead_refs, lambda _: slice(at, at + width))
            out_ref[:, at : at + width] = low(dot_left(hidden_all, grad_all))

    return run(kernel, [*ahead, *grads], [shaped((width, units), BF)])[0]


def up_changes(ahead, pres, units, width):
    cols = len(ahead)

    def kernel(*refs):
        ahead_refs, pre_refs, out_ref = refs[:cols], refs[cols : 2 * cols], refs[2 * cols]
        pre_all = gathered(pre_refs)
        out_ref[:width, :] = low(dot_left(slices_of(ahead_refs, units, width), pre_all))
        total = jnp.sum(wide(pre_all), axis=0, keepdims=True)
        out_ref[width:, :] = low(jnp.broadcast_to(total, (16, units)))

    return run(kernel, [*ahead, *pres], [shaped((width + 16, units), BF)])[0]


def attention_changes(ahead, joined, across, width, middles=None):
    cols = len(ahead)

    def kernel(*refs):
        ahead_refs, joined_refs, out_refs = refs[:cols], refs[cols : 2 * cols], refs[2 * cols :]
        out_ref = out_refs[0]
        joined_all = rows_of(joined_refs, lambda _: slice(0, 3 * across))
        out_ref[:width, : 3 * across] = low(
            dot_left(slices_of(ahead_refs, across, width), joined_all)
        )
        total = jnp.sum(wide(joined_all), axis=0, keepdims=True)
        out_ref[width:, : 3 * across] = low(jnp.broadcast_to(total, (16, 3 * across)))
        if middles is None:
            output_part(ahead_refs, joined_refs, 3 * across, out_ref, 3 * across)
            out_ref[width:, 3 * across :] = jnp.zeros((16, out_ref.shape[1] - 3 * across), BF)

    def output_part(ahead_refs, middle_refs, shared, out_ref, column):
        mixed_all = rows_of(ahead_refs, lambda _: slice(0, across))
        change = low(dot_left(mixed_all, slices_of(middle_refs, shared, width)))
        for at in range(0, across, width):
            out_ref[:width, column + at : column + at + width] = change[at : at + width]

    columns = 3 * across if middles else 4 * across
    return run(kernel, [*ahead, *joined], [shaped((width + 16, columns), BF)])[0]


def output_changes(ahead, middles, across, width):
    cols = len(ahead)

    def kernel(*refs):
        mixed_all = rows_of(refs[:cols], lambda _: slice(0, across))
        change = low(dot_left(mixed_all, slices_of(refs[cols : 2 * cols], 0, width)))
        for at in range(0, across, width):
            refs[-1][:, at : at + width] = change[at : at + width]

    return run(kernel, [*ahead, *middles], [shaped((width, across), BF)])[0]


def finish(own, other, layer, cuts, shapes, kept, line):
    width = own.shape[0] - (16 if line else 0)

    def kernel(own_ref, other_ref, *refs):
        out_refs = refs[len(kept or ()) :]
        for out_ref, pieces in zip(out_refs, cuts):
            row = 0
            for start, stop in pieces:
                out_ref[0, row : row + width, :] = wide(own_ref[:width, start:stop]) + wide(
                    other_ref[:width, start:stop]
                )
                row += width
        if line:
            out_refs[-1][...] = wide(own_ref[width : width + 8, :]) + wide(
                other_ref[width : width + 8, :]
            )

    def whole(array):
        return pl.BlockSpec(array.shape, lambda at: (0, 0))

    lines = [shaped((8, own.shape[1]), F32)] if line else []
    return pl.pallas_call(
        kernel,
        grid=(1,),
        in_specs=[whole(own), whole(other)] + [ANY] * len(kept or ()),
        out_specs=[pl.BlockSpec((1,) + shape[1:], lambda at: (layer, 0, 0)) for shape in shapes]
        + [whole(array) for array in lines],
        out_shape=[shaped(shape, F32) for shape in shapes] + lines,
        input_output_aliases={2 + at: at for at in range(len(kept or ()))},
        compiler_params=pltpu.CompilerParams(vmem_limit_bytes=VMEM_LIMIT),
    )(own, other, *(kept or ()))


def finish_vectors(own, other, up_lines, joined_lines, across):
    width = own.shape[1]
    units = up_lines[0].shape[1]
    heads = across // HD

    def kernel(*refs):
        own_ref, other_ref = refs[:2]
        up_refs = refs[2 : 2 + LAYERS]
        joined_refs = refs[2 + LAYERS : 2 + 2 * LAYERS]
        outs = refs[2 + 2 * LAYERS :]
        total = own_ref[...] + other_ref[...]
        for layer in range(LAYERS):
            here = slice(layer, layer + 1)
            for slot in range(6):
                outs[slot][here, :] = total[6 * layer + slot : 6 * layer + slot + 1, :]
            outs[6][here, :] = up_refs[layer][:1, :]
            for head in range(heads):
                at = head * 3 * HD
                there = slice(head * HD, (head + 1) * HD)
                outs[7][here, there] = joined_refs[layer][:1, at : at + HD]
                outs[8][here, there] = joined_refs[layer][:1, at + 2 * HD : at + 3 * HD]

    return run(
        kernel,
        [own, other, *up_lines, *joined_lines],
        [shaped((LAYERS, width), F32)] * 6
        + [shaped((LAYERS, units), F32)]
        + [shaped((LAYERS, across), F32)] * 2,
    )


def turn(blocks):
    got = turn_blocks(spread(blocks, ROW))
    return trade(got, COL)


def turn_sum(blocks, dtype, extra=0):
    got = turn_blocks(trade(blocks, COL), extra)
    return sum_blocks(trade(got, ROW), dtype, extra)


def sum_blocks(got, dtype, extra):
    rows, width = got[0].shape[0] - extra, got[0].shape[1]

    def kernel(*refs):
        parts = refs[: len(got)]
        total = tree_sum([wide(ref[:rows, :]) for ref in parts])
        refs[len(got)][...] = total.astype(dtype)
        if extra:
            refs[len(got) + 1][...] = tree_sum([wide(ref[rows:, :]) for ref in parts])

    outs = [shaped((rows, width), dtype)]
    if extra:
        outs.append(shaped((extra, width), F32))
    return run(kernel, list(got), outs)


def shards(
    block_input,
    cotangent,
    first_gain,
    first_shift,
    joined_weight,
    query_bias,
    value_bias,
    output_weight,
    output_bias,
    second_gain,
    second_shift,
    upward_weight,
    upward_bias,
    downward_weight,
    downward_bias,
):
    across = query_bias.shape[1]
    units = upward_bias.shape[1]
    width = block_input.shape[1]
    size, cols = lax.axis_size(ROW), lax.axis_size(COL)
    steps = sends_of(cols)

    def exchange(sends):
        return [sends[0]] + relay(dict(zip(steps, sends[1:])), COL)

    vectors, (query_bias, value_bias, upward_bias) = start_vectors(
        [first_gain, first_shift, output_bias, second_gain, second_shift, downward_bias],
        [query_bias, value_bias, upward_bias],
    )
    vecs = relay_all(vectors, COL)
    weights = []
    for layer in range(LAYERS):
        weights.append([])
        for first in (True, False):
            pair = (joined_weight, output_weight) if first else (upward_weight, downward_weight)
            pack = pack_weights(*pair, layer, width, first)
            weights[layer].append(relay_all(pack, COL))
    got = turn(block_input)
    grad_blocks = row_blocks(turn(cotangent), size)
    resid, last_kept, input_blocks = first_norm(got, vecs, size)
    stats = None
    saved = []
    for layer in range(LAYERS):
        attention_packs, feed_packs = weights[layer]
        first_kept = (resid, stats)
        (qkv, probs), parts, sends = attention_forward(
            spread(norm_input, ROW) if layer else input_blocks,
            attention_packs,
            query_bias,
            value_bias,
            layer,
        )
        attention_ahead = exchange(sends)
        middle, norm_input, stats = next_norm(
            resid, trade(parts, ROW), vecs, layer, BIAS_OUT, GAIN_TWO, SHIFT_TWO
        )
        second_kept = (middle, stats)
        slope, parts, sends = feed_forward(
            spread(norm_input, ROW),
            feed_packs,
            upward_bias,
            layer,
            *((middle, vecs) if layer + 1 == LAYERS else ()),
        )
        feed_ahead = exchange(sends)
        saved.append((first_kept, second_kept, qkv, probs, slope, attention_ahead, feed_ahead))
        if layer + 1 < LAYERS:
            resid, norm_input, stats = next_norm(
                middle, trade(parts, ROW), vecs, layer, BIAS_DOWN, GAIN_ONE, SHIFT_ONE
            )
        else:
            (block_output,) = turn_sum(parts, BF)

    grad_resid = grad_blocks[0]
    sums = []
    down_outs = up_outs = joined_out = output_out = None
    up_lines, joined_lines = [None] * LAYERS, [None] * LAYERS
    for layer in reversed(range(LAYERS)):
        attention_packs, feed_packs = weights[layer]
        first_kept, second_kept, qkv, probs, slope, attention_ahead, feed_ahead = saved[layer]
        parts, grad_pre, sends = feed_backward(grad_blocks, feed_packs, slope)
        grads = exchange(sends)
        pres = relay_all(grad_pre, COL)
        grad_middle, middle_low, second_sums = norm_backward(
            grad_resid, trade(parts, ROW), *second_kept, vecs, layer, GAIN_TWO, True
        )
        blocks = spread(middle_low, ROW)
        middles = None
        if not layer:
            middles = exchange(bundle_blocks(blocks, cols))
        parts, sends = attention_backward(
            blocks,
            attention_packs,
            qkv,
            probs,
            attention_ahead[0],
            across,
            None if layer else (last_kept, grad_middle, vecs, [second_sums] + sums),
        )
        joined = exchange(sends) if layer else relay_all(sends[0], COL)
        if layer:
            grad_resid, grad_low, first_sums = norm_backward(
                grad_middle, trade(parts, ROW), *first_kept, vecs, layer, GAIN_ONE, False
            )
            grad_blocks = spread(grad_low, ROW)
            sums = [first_sums, second_sums] + sums
        else:
            input_gradient, totals = turn_sum(parts, F32, 16)
        change = down_changes(feed_ahead, grads, units, width)
        down_outs = finish(
            change,
            axis_swap(change, DP, 1),
            layer,
            [[(at, at + width) for at in range(0, units, width)]],
            [downward_weight.shape],
            down_outs,
            False,
        )
        change = up_changes(feed_ahead, pres, units, width)
        *up_outs, up_lines[layer] = finish(
            change,
            axis_swap(change, DP, 1),
            layer,
            [[(0, units)]],
            [upward_weight.shape],
            up_outs,
            True,
        )
        change = attention_changes(attention_ahead, joined, across, width, middles)
        output_cut = [(at, at + width) for at in range(0, across, width)]
        if layer:
            joined_out, output_out, joined_lines[layer] = finish(
                change,
                axis_swap(change, DP, 1),
                layer,
                [[(0, 3 * across)], [(3 * across + one, 3 * across + two) for one, two in output_cut]],
                [joined_weight.shape, output_weight.shape],
                None,
                True,
            )
        else:
            joined_out, joined_lines[layer] = finish(
                change,
                axis_swap(change, DP, 1),
                layer,
                [[(0, 3 * across)]],
                [joined_weight.shape],
                [joined_out],
                True,
            )
            change = output_changes(attention_ahead, middles, across, width)
            (output_out,) = finish(
                change,
                axis_swap(change, DP, 1),
                layer,
                [output_cut],
                [output_weight.shape],
                [output_out],
                False,
            )
    vector_sums = finish_vectors(totals, axis_swap(totals, DP, 1), up_lines, joined_lines, across)
    return (
        block_output,
        input_gradient,
        vector_sums[0],
        vector_sums[1],
        joined_out,
        vector_sums[7],
        vector_sums[8],
        output_out,
        vector_sums[4],
        vector_sums[2],
        vector_sums[3],
        up_outs[0],
        vector_sums[6],
        down_outs[0],
        vector_sums[5],
    )


def solution(mesh):
    return jax.shard_map(
        shards,
        mesh=mesh,
        in_specs=(
            P((DP, ROW), COL),
            P((DP, ROW), COL),
            P(None, COL),
            P(None, COL),
            P(None, COL, ROW),
            P(None, ROW),
            P(None, ROW),
            P(None, ROW, COL),
            P(None, COL),
            P(None, COL),
            P(None, COL),
            P(None, COL, ROW),
            P(None, ROW),
            P(None, ROW, COL),
            P(None, COL),
        ),
        out_specs=(
            P((DP, ROW), COL),
            P((DP, ROW), COL),
            P(None, COL),
            P(None, COL),
            P(None, COL, ROW),
            P(None, ROW),
            P(None, ROW),
            P(None, ROW, COL),
            P(None, COL),
            P(None, COL),
            P(None, COL),
            P(None, COL, ROW),
            P(None, ROW),
            P(None, ROW, COL),
            P(None, COL),
        ),
        check_vma=False,
    )
```

```python
import math

import jax
import jax.numpy as jnp
from jax import lax
from jax.experimental import pallas as pl
from jax.experimental.pallas import tpu as pltpu
from jax.sharding import PartitionSpec as P


H = 16
HD = 64
LAYERS = 2

VMEM_LIMIT = 16 * 1024 * 1024
DP, ROW, COL = "dp", "row", "col"
GAIN_ONE, SHIFT_ONE, BIAS_OUT, GAIN_TWO, SHIFT_TWO, BIAS_DOWN = range(6)

norm_epsilon = 1e-05
gelu_coef = 0.044715
gelu_scale = math.sqrt(2.0 / math.pi)
masked_score = -1e30


def int_log2(value):
    return value.bit_length() - 1


def axis_swap(local, axis, step):
    size = lax.axis_size(axis)
    return lax.ppermute(local, axis, [(place, place ^ step) for place in range(size)])


def spread(local, axis):
    size = lax.axis_size(axis)
    return [local] + [axis_swap(local, axis, step) for step in range(1, size)]


def trade(blocks, axis):
    return [blocks[0]] + [axis_swap(blocks[step], axis, step) for step in range(1, len(blocks))]


def relay(sends, axis):
    size = lax.axis_size(axis)
    got = {}
    step = size // 2
    while step:
        arrived = {place ^ step: axis_swap(got[place], axis, step) for place in sorted(got)}
        arrived[step] = axis_swap(sends[step], axis, step)
        got.update(arrived)
        step //= 2
    return [got[place] for place in range(1, size)]


def sends_of(size):
    steps = []
    step = 1
    while step < size:
        steps.append(step)
        step *= 2
    return steps


def relay_all(local, axis):
    return [local] + relay({step: local for step in sends_of(lax.axis_size(axis))}, axis)


def high_bit(place):
    return 1 << int_log2(place)


def tree_sum(parts):
    parts = list(parts)
    while len(parts) > 1:
        parts = [parts[at] + parts[at + 1] for at in range(0, len(parts), 2)]
    return parts[0]


def dot(left, right):
    return lax.dot_general(left, right, (((1,), (0,)), ((), ())), preferred_element_type=jnp.float32)


def dot_right(left, right):
    return lax.dot_general(left, right, (((1,), (1,)), ((), ())), preferred_element_type=jnp.float32)


def dot_left(left, right):
    return lax.dot_general(left, right, (((0,), (0,)), ((), ())), preferred_element_type=jnp.float32)


def low(values):
    return values.astype(jnp.bfloat16)


def wide(values):
    return values.astype(jnp.float32)


def shaped(shape, dtype):
    return jax.ShapeDtypeStruct(shape, dtype)


BF = jnp.bfloat16
F32 = jnp.float32


VMEM = pl.BlockSpec(memory_space=pltpu.VMEM)
ANY = pl.BlockSpec(memory_space=pl.ANY)
HBM = pl.BlockSpec(memory_space=pltpu.HBM)


def run(kernel, arrays, outs, scratch=(), spec=None):
    return pl.pallas_call(
        kernel,
        in_specs=[spec or VMEM] * len(arrays),
        out_specs=[VMEM] * len(outs),
        out_shape=outs,
        scratch_shapes=list(scratch),
        compiler_params=pltpu.CompilerParams(vmem_limit_bytes=VMEM_LIMIT),
    )(*arrays)


def vector_row(vecs, at):
    return jnp.concatenate([vec[at : at + 1, :] for vec in vecs], axis=1)


def norm_into(resid, gain, shift, input_ref, stats_ref):
    mean = jnp.mean(resid, axis=1, keepdims=True)
    spread_out = jnp.mean(resid * resid, axis=1, keepdims=True) - mean * mean
    scale = lax.rsqrt(spread_out + norm_epsilon)
    half = stats_ref.shape[1] // 2
    stats_ref[:, :half] = jnp.broadcast_to(mean, (resid.shape[0], half))
    stats_ref[:, half:] = jnp.broadcast_to(scale, (resid.shape[0], half))
    input_ref[...] = low((resid - mean) * scale * gain + shift)


def start_copies(copies):
    for copy in copies:
        copy.start()
    for copy in copies:
        copy.wait()


def in_hbm(array):
    return pltpu.with_memory_space_constraint(array, pltpu.HBM)


def weight_pieces(upward, downward, layer, width, first):
    if first:
        return [(0, (layer,), upward), (1, (layer,), downward)]
    chunks = downward[1] // width
    pieces = [(0, (layer,), upward[2])]
    for at in range(chunks):
        pieces.append((1, (layer, slice(at * width, (at + 1) * width)), downward[2]))
    return pieces


def pack_copies(refs, out_ref, sems, pieces):
    copies = []
    at = 0
    for slot, (which, index, columns) in enumerate(pieces):
        copies.append(
            pltpu.make_async_copy(
                refs[which].at[index], out_ref.at[:, at : at + columns], sems.at[slot]
            )
        )
        at += columns
    return copies


def start_vectors(vectors, biases):
    count, width = len(vectors), vectors[0].shape[1]

    def kernel(*refs):
        vector_refs = refs[:count]
        bias_refs = refs[count : count + len(biases)]
        out_ref = refs[count + len(biases)]
        bias_outs = refs[count + len(biases) + 1 : count + 2 * len(biases) + 1]
        landing = refs[count + 2 * len(biases) + 1 : -1]
        sems = refs[-1]
        pairs = list(zip(vector_refs, landing)) + list(zip(bias_refs, bias_outs))
        start_copies(
            [
                pltpu.make_async_copy(source, target, sems.at[at])
                for at, (source, target) in enumerate(pairs)
            ]
        )
        for at, ref in enumerate(landing):
            out_ref[LAYERS * at : LAYERS * (at + 1), :] = ref[...]

    outs = run(
        kernel,
        [in_hbm(array) for array in (*vectors, *biases)],
        [shaped((LAYERS * count, width), F32)] + [shaped(bias.shape, F32) for bias in biases],
        [pltpu.VMEM(vector.shape, F32) for vector in vectors]
        + [pltpu.SemaphoreType.DMA((count + len(biases),))],
        HBM,
    )
    return outs[0], outs[1:]


def turn_blocks(blocks, extra=0):
    size = len(blocks)
    rows = blocks[0].shape[0] - extra

    def kernel(*refs):
        block_refs, out_refs, turn = refs[:size], refs[size : 2 * size], refs[2 * size]
        shift = lax.axis_index(ROW) ^ lax.axis_index(COL)
        for at in range(size):
            turn[at] = block_refs[at][:rows, :]
        if extra:
            total = tree_sum([wide(ref[rows:, :]) for ref in block_refs])
        for at in range(size):
            out_refs[at][:rows, :] = turn[at ^ shift]
            if extra:
                out_refs[at][rows:, :] = total.astype(out_refs[at].dtype)

    shape, dtype = blocks[0].shape, blocks[0].dtype
    return run(
        kernel,
        list(blocks),
        [shaped(shape, dtype)] * size,
        [pltpu.VMEM((size, rows, shape[1]), dtype)],
    )


def pack_weights(one, two, layer, width, first):
    last = two.shape[2] if first else two.shape
    pieces = weight_pieces(one.shape[2] if first else one.shape, last, layer, width, first)
    total = sum(piece[2] for piece in pieces)

    def kernel(one_ref, two_ref, out_ref, sems):
        start_copies(pack_copies((one_ref, two_ref), out_ref, sems, pieces))

    return pl.pallas_call(
        kernel,
        in_specs=[HBM] * 2,
        out_specs=VMEM,
        out_shape=shaped((width, total), BF),
        scratch_shapes=[pltpu.SemaphoreType.DMA((len(pieces),))],
        compiler_params=pltpu.CompilerParams(vmem_limit_bytes=VMEM_LIMIT),
    )(in_hbm(one), in_hbm(two))


def own_rows(blocks, step, rows):
    at = pl.multiple_of((lax.axis_index(ROW) ^ step) * rows, rows)
    return jnp.concatenate([ref[pl.ds(at, rows), :] for ref in blocks], axis=1)


def first_norm(got, vecs, size):
    cols = len(got)
    length, width = got[0].shape
    rows, full = length // size, width * cols

    def kernel(*refs):
        got_refs = refs[:cols]
        vec_refs = refs[cols : 2 * cols]
        resid_ref, normed_ref, scale_ref = refs[2 * cols : 2 * cols + 3]
        input_refs = refs[2 * cols + 3 :]
        gain = vector_row(vec_refs, GAIN_ONE * LAYERS)
        shift = vector_row(vec_refs, SHIFT_ONE * LAYERS)
        for step in range(size):
            here = slice(step * rows, (step + 1) * rows)
            resid = wide(own_rows(got_refs, step, rows))
            if not step:
                resid_ref[...] = resid
            mean = jnp.mean(resid, axis=1, keepdims=True)
            spread_out = jnp.mean(resid * resid, axis=1, keepdims=True) - mean * mean
            scale = lax.rsqrt(spread_out + norm_epsilon)
            normed = (resid - mean) * scale
            normed_ref[here, :] = normed
            scale_ref[here, :] = jnp.broadcast_to(scale, (rows, 128))
            input_refs[step][...] = low(normed * gain + shift)

    outs = run(
        kernel,
        [*got, *vecs],
        [shaped((rows, full), F32), shaped((length, full), F32), shaped((length, 128), F32)]
        + [shaped((rows, full), BF)] * size,
    )
    return outs[0], (outs[1], outs[2]), outs[3:]


def row_blocks(got, size):
    length, width = got[0].shape
    rows, cols = length // size, len(got)
    steps = sends_of(cols)

    def kernel(*refs):
        whole = [own_rows(refs[:cols], step, rows) for step in range(size)]
        for step, value in enumerate(whole):
            refs[cols + step][...] = value
        whole = jnp.concatenate(whole, axis=0)
        bundle_into(refs[cols + size :], steps, [], [whole], width)

    outs = run(
        kernel,
        list(got),
        [shaped((rows, width * cols), BF)] * size + bundle_shapes(length, steps, 0, 1, width),
    )
    return outs[:size], outs[size:]


def next_norm(resid, parts, vecs, layer, bias_at, gain_at, shift_at):
    count = len(parts)
    next_layer = layer + 1 if gain_at == GAIN_ONE else layer

    def kernel(resid_ref, *refs):
        part_refs = refs[:count]
        vec_refs = refs[count : count + len(vecs)]
        out_ref, input_ref, stats_ref = refs[count + len(vecs) :]
        total = tree_sum([wide(ref[...]) for ref in part_refs])
        resid = resid_ref[...] + total + vector_row(vec_refs, bias_at * LAYERS + layer)
        out_ref[...] = resid
        norm_into(
            resid,
            vector_row(vec_refs, gain_at * LAYERS + next_layer),
            vector_row(vec_refs, shift_at * LAYERS + next_layer),
            input_ref,
            stats_ref,
        )

    rows, full = resid.shape
    return run(
        kernel,
        [resid, *parts, *vecs],
        [shaped((rows, full), F32), shaped((rows, full), BF), shaped((rows, 256), F32)],
    )


def cut_rows(value, refs):
    rows = refs[0].shape[0]
    for at, ref in enumerate(refs):
        ref[...] = value[at * rows : (at + 1) * rows]


def cut_turned(partial, ours, refs):
    rows, width = ours.shape[0], refs[0].shape[1]
    for step in range(partial.shape[0] // rows):
        block = partial[step * rows : (step + 1) * rows]
        if not step:
            block = block + ours
        at = pl.multiple_of((lax.axis_index(ROW) ^ step) * rows, rows)
        for place, ref in enumerate(refs):
            ref[pl.ds(at, rows), :] = low(block[:, place * width : (place + 1) * width])


def gathered(refs):
    return jnp.concatenate([ref[...] for ref in refs], axis=0)


def attention_forward(blocks, packs, query_bias, value_bias, layer):
    size, cols = len(blocks), len(packs)
    rows, full = blocks[0].shape
    length = size * rows
    width = full // cols
    across = query_bias.shape[1]
    heads = across // HD
    shift = int_log2(rows)
    steps = sends_of(cols)

    def kernel(*refs):
        block_refs = refs[:size]
        pack_refs = refs[size : size + cols]
        query_bias_ref, value_bias_ref = refs[size + cols : size + cols + 2]
        qkv_ref, probs_ref = refs[size + cols + 2 : size + cols + 4]
        part_refs = refs[size + cols + 4 : 2 * size + cols + 4]
        send_refs = refs[2 * size + cols + 4 :]
        mixed_ref = send_refs[0]
        full_first = gathered(block_refs)
        joined = tree_sum(
            [
                dot(full_first[:, at * width : (at + 1) * width], pack_refs[at][:, : 3 * across])
                for at in range(cols)
            ]
        )
        row = lax.axis_index(ROW)

        def where_is(axis):
            index = lax.broadcasted_iota(jnp.int32, (length, length), axis)
            return ((lax.shift_right_logical(index, shift) ^ row) << shift) + (index & (rows - 1))

        offset = wide(where_is(1) - where_is(0))
        allowed = offset <= 0.0
        for head in range(heads):
            at = head * 3 * HD
            here = slice(head * HD, (head + 1) * HD)
            query = low(joined[:, at : at + HD] + query_bias_ref[layer : layer + 1, here])
            keys = low(joined[:, at + HD : at + 2 * HD])
            values = low(
                joined[:, at + 2 * HD : at + 3 * HD] + value_bias_ref[layer : layer + 1, here]
            )
            qkv_ref[:, at : at + HD] = query
            qkv_ref[:, at + HD : at + 2 * HD] = keys
            qkv_ref[:, at + 2 * HD : at + 3 * HD] = values
            index = jnp.full((1, length), row * heads + head + 1, jnp.int32)
            slope = jnp.exp2(wide(index) * (-8.0 / H))
            scores = dot_right(query, keys) * (1.0 / math.sqrt(HD)) + slope * offset
            scores = jnp.where(allowed, scores, masked_score)
            top = jnp.max(scores, axis=1, keepdims=True)
            log_total = top + jnp.log(jnp.sum(jnp.exp(scores - top), axis=1, keepdims=True))
            probs = jnp.exp(scores - log_total)
            probs_ref[head] = probs
            mixed_ref[:, here] = low(dot(low(probs), values))
        mixed = mixed_ref[:, :across]
        partial = jnp.concatenate(
            [low(dot(mixed, pack_ref[:, 3 * across : 3 * across + width])) for pack_ref in pack_refs],
            axis=1,
        )
        cut_rows(partial, part_refs)
        bundle_into(send_refs, steps, [mixed], [full_first], width)

    outs = run(
        kernel,
        [*blocks, *packs, query_bias, value_bias],
        [shaped((length, 3 * across), BF), shaped((heads, length, length), F32)]
        + [shaped((rows, full), BF)] * size
        + bundle_shapes(length, steps, across, 1, width),
    )
    return outs[:2], outs[2 : 2 + size], outs[2 + size :]


def bundle_into(refs, steps, shared, addressed, width):
    for at, ref in enumerate(refs):
        first = steps[at - 1] if at else 0
        count = first if at else 1
        column = 0
        for value in shared:
            ref[:, column : column + value.shape[1]] = value
            column += value.shape[1]
        for place in range(first, first + count):
            for value in addressed:
                ref[:, column : column + width] = value[:, place * width : (place + 1) * width]
                column += width


def bundle_shapes(length, steps, shared, addressed, width):
    counts = [1] + list(steps)
    return [shaped((length, shared + count * addressed * width), BF) for count in counts]


def feed_forward(blocks, packs, upward_bias, layer, middle=None, vecs=()):
    size, cols = len(blocks), len(packs)
    rows, full = blocks[0].shape
    length = size * rows
    width = full // cols
    units = upward_bias.shape[1]
    steps = sends_of(cols)
    extra = [middle, *vecs] if vecs else []
    parts = [shaped((length, width), BF)] * cols if vecs else [shaped((rows, full), BF)] * size

    def kernel(*refs):
        block_refs = refs[:size]
        pack_refs = refs[size : size + cols]
        bias_ref = refs[size + cols]
        more = refs[size + cols + 1 : size + cols + 1 + len(extra)]
        slope_ref = refs[size + cols + 1 + len(extra)]
        part_refs = refs[size + cols + 2 + len(extra) :][: len(parts)]
        send_refs = refs[size + cols + 2 + len(extra) + len(parts) :]
        full_second = gathered(block_refs)
        pre_act = tree_sum(
            [
                dot(full_second[:, at * width : (at + 1) * width], pack_refs[at][:, :units])
                for at in range(cols)
            ]
        )
        pre_act = pre_act + bias_ref[layer : layer + 1, :]
        inner = gelu_scale * (pre_act + gelu_coef * pre_act * pre_act * pre_act)
        tangent = jnp.tanh(inner)
        hidden = low(0.5 * pre_act * (1.0 + tangent))
        slope_ref[...] = 0.5 * (1.0 + tangent) + 0.5 * pre_act * (
            1.0 - tangent * tangent
        ) * gelu_scale * (1.0 + 3.0 * gelu_coef * pre_act * pre_act)
        partial = jnp.concatenate(
            [
                tree_sum(
                    [
                        dot(
                            hidden[:, at : at + width],
                            pack_ref[:, units + at : units + at + width],
                        )
                        for at in range(0, units, width)
                    ]
                )
                for pack_ref in pack_refs
            ],
            axis=1,
        )
        if vecs:
            bias = vector_row(more[1:], BIAS_DOWN * LAYERS + layer)
            cut_turned(partial, more[0][...] + bias, part_refs)
        else:
            cut_rows(low(partial), part_refs)
        bundle_into(send_refs, steps, [hidden], [full_second], width)

    outs = run(
        kernel,
        [*blocks, *packs, upward_bias, *extra],
        [shaped((length, units), F32)]
        + parts
        + bundle_shapes(length, steps, units, 1, width),
    )
    return outs[0], outs[1 : 1 + len(parts)], outs[1 + len(parts) :]


def feed_backward(blocks, packs, slope):
    size, cols = len(blocks), len(packs)
    rows, full = blocks[0].shape
    length = size * rows
    width = full // cols
    units = slope.shape[1]

    def kernel(*refs):
        block_refs = refs[:size]
        pack_refs = refs[size : size + cols]
        slope_ref = refs[size + cols]
        part_refs = refs[size + cols + 1 : 2 * size + cols + 1]
        pre_ref = refs[2 * size + cols + 1]
        full_grad = gathered(block_refs)
        grad_hidden = jnp.concatenate(
            [
                tree_sum(
                    [
                        dot_right(
                            full_grad[:, place * width : (place + 1) * width],
                            pack_refs[place][:, units + at : units + at + width],
                        )
                        for place in range(cols)
                    ]
                )
                for at in range(0, units, width)
            ],
            axis=1,
        )
        grad_pre = low(grad_hidden * slope_ref[...])
        pre_ref[...] = grad_pre
        partial = jnp.concatenate(
            [low(dot_right(grad_pre, pack_ref[:, :units])) for pack_ref in pack_refs], axis=1
        )
        cut_rows(partial, part_refs)

    outs = run(
        kernel,
        [*blocks, *packs, slope],
        [shaped((rows, full), BF)] * size
        + [shaped((length, units), BF)],
    )
    return outs[:size], outs[size]


def bundle_blocks(blocks, cols):
    rows, full = blocks[0].shape
    width = full // cols
    steps = sends_of(cols)

    def kernel(*refs):
        bundle_into(refs[len(blocks) :], steps, [], [gathered(refs[: len(blocks)])], width)

    return run(kernel, list(blocks), bundle_shapes(len(blocks) * rows, steps, 0, 1, width))


def norm_back_math(grad_in, part_refs, resid_ref, stats_ref, gain):
    grad_out = tree_sum([wide(ref[...]) for ref in part_refs])
    half = stats_ref.shape[1] // 2
    scale = stats_ref[:, half : half + 1]
    normed = (resid_ref[...] - stats_ref[:, :1]) * scale
    grad_normed = grad_out * gain
    first = jnp.mean(grad_normed, axis=1, keepdims=True)
    second = jnp.mean(grad_normed * normed, axis=1, keepdims=True)
    total = grad_in + scale * (grad_normed - first - normed * second)
    sums = [
        jnp.sum(grad_out * normed, axis=0, keepdims=True),
        jnp.sum(grad_out, axis=0, keepdims=True),
    ]
    return total, sums


def norm_backward(grad_resid, parts, resid, stats, vecs, layer, gain_at, extra):
    count = len(parts)
    rows, full = grad_resid.shape

    def kernel(grad_ref, resid_ref, stats_ref, *refs):
        part_refs = refs[:count]
        vec_refs = refs[count : count + len(vecs)]
        out_ref, low_ref, sums_ref = refs[count + len(vecs) :]
        grad_in = wide(grad_ref[...])
        total, sums = norm_back_math(
            grad_in, part_refs, resid_ref, stats_ref, vector_row(vec_refs, gain_at * LAYERS + layer)
        )
        out_ref[...] = total
        low_ref[...] = low(total)
        if extra:
            sums.append(jnp.sum(total, axis=0, keepdims=True))
            sums.append(jnp.sum(grad_in, axis=0, keepdims=True))
        for at, value in enumerate(sums):
            sums_ref[at : at + 1, :] = value

    return run(
        kernel,
        [grad_resid, resid, stats, *parts, *vecs],
        [
            shaped((rows, full), F32),
            shaped((rows, full), BF),
            shaped((4 if extra else 2, full), F32),
        ],
    )


def attention_backward(blocks, packs, qkv, probs, mixed, across, last=None):
    size, cols = len(blocks), len(packs)
    rows, full = blocks[0].shape
    length = size * rows
    width = full // cols
    heads = across // HD
    factor = 1.0 / math.sqrt(HD)

    extra = []
    parts = [shaped((rows, full), BF)] * size
    sends = bundle_shapes(length, sends_of(cols), 3 * across, 1, width)
    if last:
        sends = [shaped((length, 3 * across), BF)]
        kept, grad_middle, vecs, other_sums = last
        extra = [*kept, grad_middle, *vecs, *other_sums]
        parts = [shaped((length + 16, width), BF)] * cols

    def kernel(*refs):
        block_refs = refs[:size]
        pack_refs = refs[size : size + cols]
        qkv_ref, probs_ref, mixed_ref = refs[size + cols : size + cols + 3]
        more = refs[size + cols + 3 : size + cols + 3 + len(extra)]
        part_refs = refs[size + cols + 3 + len(extra) :][: len(parts)]
        send_refs = refs[size + cols + 3 + len(extra) + len(parts) :]
        joined_ref = send_refs[0]
        full_middle = gathered(block_refs)
        grad_mixed = low(
            tree_sum(
                [
                    dot_right(
                        full_middle[:, at * width : (at + 1) * width],
                        pack_refs[at][:, 3 * across : 3 * across + width],
                    )
                    for at in range(cols)
                ]
            )
        )
        for head in range(heads):
            at = head * 3 * HD
            here = slice(head * HD, (head + 1) * HD)
            query = qkv_ref[:, at : at + HD]
            keys = qkv_ref[:, at + HD : at + 2 * HD]
            values = qkv_ref[:, at + 2 * HD : at + 3 * HD]
            grad_here = grad_mixed[:, here]
            probs = probs_ref[head]
            value_sum = dot_left(low(probs), grad_here)
            grad_probs = dot_right(grad_here, values)
            delta = jnp.sum(wide(grad_here) * wide(mixed_ref[:, here]), axis=1, keepdims=True)
            grad_scores = low(probs * (grad_probs - delta))
            joined_ref[:, at : at + HD] = low(dot(grad_scores, keys) * factor)
            joined_ref[:, at + HD : at + 2 * HD] = low(dot_left(grad_scores, query) * factor)
            joined_ref[:, at + 2 * HD : at + 3 * HD] = low(value_sum)
        grad_joined = joined_ref[:, : 3 * across]
        partial = jnp.concatenate(
            [dot_right(grad_joined, pack_ref[:, : 3 * across]) for pack_ref in pack_refs],
            axis=1,
        )
        if last:
            normed, scale = more[0][...], more[1][:, :1]
            grad_normed = partial * vector_row(more[3 : 3 + cols], GAIN_ONE * LAYERS)
            first = jnp.mean(grad_normed, axis=1, keepdims=True)
            second = jnp.mean(grad_normed * normed, axis=1, keepdims=True)
            cut_turned(
                scale * (grad_normed - first - normed * second), more[2][...], part_refs
            )
            lines = [
                jnp.sum(partial * normed, axis=0, keepdims=True),
                jnp.sum(partial, axis=0, keepdims=True),
            ]
            for ref in more[3 + cols :]:
                lines += [ref[at : at + 1, :] for at in range(ref.shape[0])]
            lines.append(jnp.zeros((16 - len(lines), full), F32))
            lines = low(jnp.concatenate(lines, axis=0))
            for place, ref in enumerate(part_refs):
                ref[length:, :] = lines[:, place * width : (place + 1) * width]
        else:
            cut_rows(low(partial), part_refs)
        if not last:
            bundle_into(send_refs, sends_of(cols), [grad_joined], [full_middle], width)

    outs = run(
        kernel,
        [*blocks, *packs, qkv, probs, mixed, *extra],
        parts + sends,
    )
    return outs[: len(parts)], outs[len(parts) :]


def rows_of(refs, pick):
    return jnp.concatenate([ref[:, pick(at)] for at, ref in enumerate(refs)], axis=0)


def slices_of(refs, shared, width):
    def pick(place):
        start = shared + (place - high_bit(place) if place else 0) * width
        return slice(start, start + width)

    return rows_of(refs, pick)


def down_changes(ahead, grads, units, width):
    cols = len(ahead)

    def kernel(*refs):
        ahead_refs, grad_refs, out_ref = refs[:cols], refs[cols : 2 * cols], refs[2 * cols]
        grad_all = slices_of(grad_refs, 0, width)
        for at in range(0, units, width):
            hidden_all = rows_of(ahead_refs, lambda _: slice(at, at + width))
            out_ref[:, at : at + width] = low(dot_left(hidden_all, grad_all))

    return run(kernel, [*ahead, *grads], [shaped((width, units), BF)])[0]


def up_changes(ahead, pres, units, width):
    cols = len(ahead)

    def kernel(*refs):
        ahead_refs, pre_refs = refs[:cols], refs[cols : 2 * cols]
        pre_all = gathered(pre_refs)
        refs[-2][...] = low(dot_left(slices_of(ahead_refs, units, width), pre_all))
        refs[-1][...] = jnp.sum(wide(pre_all), axis=0, keepdims=True)

    return run(kernel, [*ahead, *pres], [shaped((width, units), BF), shaped((1, units), F32)])


def attention_changes(ahead, joined, across, width, middles=None):
    cols = len(ahead)

    def kernel(*refs):
        ahead_refs, joined_refs, out_refs = refs[:cols], refs[cols : 2 * cols], refs[2 * cols :]
        out_ref = out_refs[0]
        joined_all = rows_of(joined_refs, lambda _: slice(0, 3 * across))
        out_ref[:, : 3 * across] = low(dot_left(slices_of(ahead_refs, across, width), joined_all))
        out_refs[1][...] = jnp.sum(wide(joined_all), axis=0, keepdims=True)
        if middles is None:
            output_part(ahead_refs, joined_refs, 3 * across, out_ref, 3 * across)

    def output_part(ahead_refs, middle_refs, shared, out_ref, column):
        mixed_all = rows_of(ahead_refs, lambda _: slice(0, across))
        change = low(dot_left(mixed_all, slices_of(middle_refs, shared, width)))
        for at in range(0, across, width):
            out_ref[:, column + at : column + at + width] = change[at : at + width]

    columns = 3 * across if middles else 4 * across
    return run(
        kernel, [*ahead, *joined], [shaped((width, columns), BF), shaped((1, 3 * across), F32)]
    )


def output_changes(ahead, middles, across, width):
    cols = len(ahead)

    def kernel(*refs):
        mixed_all = rows_of(refs[:cols], lambda _: slice(0, across))
        change = low(dot_left(mixed_all, slices_of(refs[cols : 2 * cols], 0, width)))
        for at in range(0, across, width):
            refs[-1][:, at : at + width] = change[at : at + width]

    return run(kernel, [*ahead, *middles], [shaped((width, across), BF)])[0]


def finish(own, other, layer, cuts, shapes, kept):
    width = own.shape[0]
    kept = kept or ()

    def kernel(own_ref, other_ref, *refs):
        for out_ref, pieces in zip(refs[len(kept) :], cuts):
            for at, (start, stop) in enumerate(pieces):
                out_ref[0, at * width : (at + 1) * width, :] = wide(own_ref[:, start:stop]) + wide(
                    other_ref[:, start:stop]
                )

    def whole(array):
        return pl.BlockSpec(array.shape, lambda at: (0, 0))

    return pl.pallas_call(
        kernel,
        grid=(1,),
        in_specs=[whole(own), whole(other)] + [ANY] * len(kept),
        out_specs=[pl.BlockSpec((1,) + shape[1:], lambda at: (layer, 0, 0)) for shape in shapes],
        out_shape=[shaped(shape, F32) for shape in shapes],
        input_output_aliases={2 + at: at for at in range(len(kept))},
        compiler_params=pltpu.CompilerParams(vmem_limit_bytes=VMEM_LIMIT),
    )(own, other, *kept)


def finish_vectors(own, other, units, across):
    width = own.shape[1]
    heads = across // HD

    def kernel(own_ref, other_ref, *outs):
        total = own_ref[...] + other_ref[...]
        row = 16

        def line(columns):
            nonlocal row
            rows = columns // width
            parts = [total[row + at : row + at + 1, :] for at in range(rows)]
            row += rows
            return jnp.concatenate(parts, axis=1)

        for layer in range(LAYERS):
            here = slice(layer, layer + 1)
            for slot in range(6):
                outs[slot][here, :] = total[6 * layer + slot : 6 * layer + slot + 1, :]
            outs[6][here, :] = line(units)
            joined = line(3 * across)
            for head in range(heads):
                at = head * 3 * HD
                there = slice(head * HD, (head + 1) * HD)
                outs[7][here, there] = joined[:, at : at + HD]
                outs[8][here, there] = joined[:, at + 2 * HD : at + 3 * HD]

    return run(
        kernel,
        [own, other],
        [shaped((LAYERS, width), F32)] * 6
        + [shaped((LAYERS, units), F32)]
        + [shaped((LAYERS, across), F32)] * 2,
    )


def turn(blocks):
    got = turn_blocks(spread(blocks, ROW))
    return trade(got, COL)


def turn_sum(blocks, dtype):
    got = turn_blocks(trade(blocks, COL))
    return sum_blocks(trade(got, ROW), dtype)


def sum_blocks(got, dtype, extra=0, lines=()):
    rows, width = got[0].shape[0] - extra, got[0].shape[1]
    below = sum(line.shape[1] for line in lines) // width
    padded = -(-(extra + below) // 8) * 8

    def kernel(*refs):
        parts = refs[: len(got)]
        line_refs = refs[len(got) : len(got) + len(lines)]
        outs = refs[len(got) + len(lines) :]
        total = tree_sum([wide(ref[:rows, :]) for ref in parts])
        outs[0][...] = total.astype(dtype)
        if extra:
            values = [tree_sum([wide(ref[rows:, :]) for ref in parts])]
            for ref in line_refs:
                values += [ref[:, at : at + width] for at in range(0, ref.shape[1], width)]
            if padded > extra + below:
                values.append(jnp.zeros((padded - extra - below, width), F32))
            outs[1][...] = jnp.concatenate(values, axis=0)

    outs = [shaped((rows, width), dtype)]
    if extra:
        outs.append(shaped((padded, width), F32))
    return run(kernel, [*got, *lines], outs)


def shards(
    block_input,
    cotangent,
    first_gain,
    first_shift,
    joined_weight,
    query_bias,
    value_bias,
    output_weight,
    output_bias,
    second_gain,
    second_shift,
    upward_weight,
    upward_bias,
    downward_weight,
    downward_bias,
):
    across = query_bias.shape[1]
    units = upward_bias.shape[1]
    width = block_input.shape[1]
    size, cols = lax.axis_size(ROW), lax.axis_size(COL)
    steps = sends_of(cols)

    def exchange(sends):
        return [sends[0]] + relay(dict(zip(steps, sends[1:])), COL)

    vectors, (query_bias, value_bias, upward_bias) = start_vectors(
        [first_gain, first_shift, output_bias, second_gain, second_shift, downward_bias],
        [query_bias, value_bias, upward_bias],
    )
    vecs = relay_all(vectors, COL)
    weights = []
    for layer in range(LAYERS):
        weights.append([])
        for first in (True, False):
            pair = (joined_weight, output_weight) if first else (upward_weight, downward_weight)
            pack = pack_weights(*pair, layer, width, first)
            weights[layer].append(relay_all(pack, COL))
    got = turn(block_input)
    grad_blocks, sends = row_blocks(turn(cotangent), size)
    grads = exchange(sends)
    resid, last_kept, input_blocks = first_norm(got, vecs, size)
    stats = None
    saved = []
    for layer in range(LAYERS):
        attention_packs, feed_packs = weights[layer]
        first_kept = (resid, stats)
        (qkv, probs), parts, sends = attention_forward(
            spread(norm_input, ROW) if layer else input_blocks,
            attention_packs,
            query_bias,
            value_bias,
            layer,
        )
        attention_ahead = exchange(sends)
        middle, norm_input, stats = next_norm(
            resid, trade(parts, ROW), vecs, layer, BIAS_OUT, GAIN_TWO, SHIFT_TWO
        )
        second_kept = (middle, stats)
        slope, parts, sends = feed_forward(
            spread(norm_input, ROW),
            feed_packs,
            upward_bias,
            layer,
            *((middle, vecs) if layer + 1 == LAYERS else ()),
        )
        feed_ahead = exchange(sends)
        saved.append((first_kept, second_kept, qkv, probs, slope, attention_ahead, feed_ahead))
        if layer + 1 < LAYERS:
            resid, norm_input, stats = next_norm(
                middle, trade(parts, ROW), vecs, layer, BIAS_DOWN, GAIN_ONE, SHIFT_ONE
            )
        else:
            (block_output,) = turn_sum(parts, BF)

    grad_resid = grad_blocks[0]
    sums = []
    down_outs = up_outs = joined_out = output_out = None
    up_lines, joined_lines = [None] * LAYERS, [None] * LAYERS
    for layer in reversed(range(LAYERS)):
        attention_packs, feed_packs = weights[layer]
        first_kept, second_kept, qkv, probs, slope, attention_ahead, feed_ahead = saved[layer]
        if not layer:
            grads = exchange(bundle_blocks(grad_blocks, cols))
        parts, grad_pre = feed_backward(grad_blocks, feed_packs, slope)
        pres = relay_all(grad_pre, COL)
        grad_middle, middle_low, second_sums = norm_backward(
            grad_resid, trade(parts, ROW), *second_kept, vecs, layer, GAIN_TWO, True
        )
        blocks = spread(middle_low, ROW)
        middles = None
        if not layer:
            middles = exchange(bundle_blocks(blocks, cols))
        parts, sends = attention_backward(
            blocks,
            attention_packs,
            qkv,
            probs,
            attention_ahead[0],
            across,
            None if layer else (last_kept, grad_middle, vecs, [second_sums] + sums),
        )
        joined = exchange(sends) if layer else relay_all(sends[0], COL)
        if layer:
            grad_resid, grad_low, first_sums = norm_backward(
                grad_middle, trade(parts, ROW), *first_kept, vecs, layer, GAIN_ONE, False
            )
            grad_blocks = spread(grad_low, ROW)
            sums = [first_sums, second_sums] + sums
        else:
            parts = trade(turn_blocks(trade(parts, COL), 16), ROW)
        change = down_changes(feed_ahead, grads, units, width)
        down_outs = finish(
            change,
            axis_swap(change, DP, 1),
            layer,
            [[(at, at + width) for at in range(0, units, width)]],
            [downward_weight.shape],
            down_outs,
        )
        change, up_lines[layer] = up_changes(feed_ahead, pres, units, width)
        up_outs = finish(
            change, axis_swap(change, DP, 1), layer, [[(0, units)]], [upward_weight.shape], up_outs
        )
        change, joined_lines[layer] = attention_changes(
            attention_ahead, joined, across, width, middles
        )
        output_cut = [(at, at + width) for at in range(0, across, width)]
        if layer:
            joined_out, output_out = finish(
                change,
                axis_swap(change, DP, 1),
                layer,
                [[(0, 3 * across)], [(3 * across + one, 3 * across + two) for one, two in output_cut]],
                [joined_weight.shape, output_weight.shape],
                None,
            )
        else:
            (joined_out,) = finish(
                change,
                axis_swap(change, DP, 1),
                layer,
                [[(0, 3 * across)]],
                [joined_weight.shape],
                [joined_out],
            )
            change = output_changes(attention_ahead, middles, across, width)
            (output_out,) = finish(
                change,
                axis_swap(change, DP, 1),
                layer,
                [output_cut],
                [output_weight.shape],
                [output_out],
            )
    lines = [line for pair in zip(up_lines, joined_lines) for line in pair]
    input_gradient, totals = sum_blocks(parts, F32, 16, lines)
    vector_sums = finish_vectors(totals, axis_swap(totals, DP, 1), units, across)
    return (
        block_output,
        input_gradient,
        vector_sums[0],
        vector_sums[1],
        joined_out,
        vector_sums[7],
        vector_sums[8],
        output_out,
        vector_sums[4],
        vector_sums[2],
        vector_sums[3],
        up_outs[0],
        vector_sums[6],
        down_outs[0],
        vector_sums[5],
    )


def solution(mesh):
    return jax.shard_map(
        shards,
        mesh=mesh,
        in_specs=(
            P((DP, ROW), COL),
            P((DP, ROW), COL),
            P(None, COL),
            P(None, COL),
            P(None, COL, ROW),
            P(None, ROW),
            P(None, ROW),
            P(None, ROW, COL),
            P(None, COL),
            P(None, COL),
            P(None, COL),
            P(None, COL, ROW),
            P(None, ROW),
            P(None, ROW, COL),
            P(None, COL),
        ),
        out_specs=(
            P((DP, ROW), COL),
            P((DP, ROW), COL),
            P(None, COL),
            P(None, COL),
            P(None, COL, ROW),
            P(None, ROW),
            P(None, ROW),
            P(None, ROW, COL),
            P(None, COL),
            P(None, COL),
            P(None, COL),
            P(None, COL, ROW),
            P(None, ROW),
            P(None, ROW, COL),
            P(None, COL),
        ),
        check_vma=False,
    )
```
